32 devices in a mesh: ctx: 16 (over z, x, core), tp: 2 (over y).
Axes of the slice: x: 2, y: 2, z: 4, core: 2. Of those that a mesh axis runs over, the one named last changes fastest.
Arguments:
- hidden_in: bfloat16 [4096, 8192], P('ctx', 'tp'), may hold values from -48 to 48
- norm_gain: float32 [8192], replicated, may hold values from 0.25 to 1.75
- w_query: bfloat16 [8192, 8192], P('ctx', 'tp'), may hold values from -0.70710678 to 0.70710678
- q_bias: bfloat16 [8192], P('tp'), may hold values from -3 to 3
- w_key: bfloat16 [8192, 1024], P('ctx', 'tp'), may hold values from -0.70710678 to 0.70710678
- key_bias: bfloat16 [1024], P('tp'), may hold values from -3 to 3
- value_weight: bfloat16 [8192, 1024], P('ctx', 'tp'), may hold values from -0.0625 to 0.0625
- value_bias: bfloat16 [1024], P('tp'), may hold values from -3 to 3
- block_segment: int32 [32], replicated, may hold values from 0 to 8, as said below
- key_blocks: int32 [32, 20], replicated, may hold values from -1 to 31, as said below
Outputs:
- attended: bfloat16 [4096, 8192], P('ctx', 'tp')
The draws below stay inside these ranges and needn't reach their ends.
Inputs may be any that keep to these rules, and one draw needn't show every extreme that they name: `block_segment`: the first 16 blocks hold segment 0; after them come responses 1 to 8 in increasing order, each of 1 to 4 blocks, one of exactly 4 blocks. `key_blocks`: row b lists in increasing order, then -1: for a prompt block, blocks 0 to b; for a response block, every prompt block and the blocks of its own response up to b.
All inputs are finite; a program needn't handle non-finite values.
Results may differ from the reference program's by a relative error of at most 0.0076.
Values may be sent and summed in bfloat16 or wider, within the bound.
No kernel may reach another device: no remote copies, remote signals or barrier semaphores. Data moves between devices by JAX's collectives and lax.ppermute only.
A program may use at most 192 MiB of HBM per device.

```python
import math
import jax
import jax.numpy as jnp
from jax import lax

MODEL_WIDTH = 8192
QUERY_HEADS = 64
KEY_VALUE_HEADS = 8
HEAD_SIZE = 128
BLK = 128
NRESP = 8
TREE_TOKENS = 4096
NB = 32
RMOST = 4
LIST = 20


def draw_hidden_in(key, part):
    row_key, column_key, noise_key = jax.random.split(key, 3)
    column_scale = jnp.exp(jax.random.uniform(column_key, (MODEL_WIDTH,), minval=math.log(0.3), maxval=math.log(3.0)))
    row_scale = jnp.exp(jax.random.uniform(row_key, (TREE_TOKENS,), minval=math.log(0.3), maxval=math.log(3.0)))
    noise = jnp.clip(jax.random.normal(noise_key, (TREE_TOKENS, MODEL_WIDTH)), -5.0, 5.0)
    value_matrix = noise * row_scale[:, None] * column_scale[None, :]
    return value_matrix.astype(jnp.bfloat16)


def drawn_weights(key):
    starting_key, query_random_key = jax.random.split(jax.random.fold_in(key, 11))
    repeat_heads = MODEL_WIDTH ** (-0.5)
    key_portion = jnp.clip(jax.random.normal(starting_key, (MODEL_WIDTH, KEY_VALUE_HEADS, HEAD_SIZE)), -6.0, 6.0) * repeat_heads
    self_portion = jnp.clip(jax.random.normal(query_random_key, (MODEL_WIDTH, KEY_VALUE_HEADS, QUERY_HEADS // KEY_VALUE_HEADS, HEAD_SIZE)), -6.0, 6.0) * repeat_heads
    query_portion = 2.0 * self_portion
    return (query_portion.reshape(MODEL_WIDTH, QUERY_HEADS * HEAD_SIZE), key_portion.reshape(MODEL_WIDTH, KEY_VALUE_HEADS * HEAD_SIZE))


def draw_w_query(key, part):
    return drawn_weights(key)[0].astype(jnp.bfloat16)


def draw_w_key(key, part):
    return drawn_weights(key)[1].astype(jnp.bfloat16)


def tree_layout(key):
    layout_key = jax.random.fold_in(key, 23)
    longest_key, grow_key = jax.random.split(layout_key)
    half = NB // 2
    answers = jnp.arange(NRESP, dtype=jnp.int32)
    longest = jax.random.randint(longest_key, (), 0, NRESP, dtype=jnp.int32)
    lengths = jnp.where(answers == longest, RMOST, 1).astype(jnp.int32)

    def grow(step, current):
        scores = jax.random.randint(jax.random.fold_in(grow_key, step), (NRESP,), 0, 1 << 20, dtype=jnp.int32) * NRESP + answers
        opened = jnp.where(current < RMOST, scores, -1)
        chosen = jnp.argmax(opened)
        return current + (answers == chosen).astype(jnp.int32)
    lengths = lax.fori_loop(0, half - RMOST - (NRESP - 1), grow, lengths)
    ends = half + jnp.cumsum(lengths).astype(jnp.int32)
    blocks = jnp.arange(NB, dtype=jnp.int32)
    segment = jnp.where(blocks < half, 0, 1 + jnp.sum((blocks[:, None] >= ends[None, :]).astype(jnp.int32), axis=1)).astype(jnp.int32)
    same = segment[:, None] == segment[None, :]
    below = blocks[None, :] <= blocks[:, None]
    allowed = (segment[None, :] == 0) & ((segment[:, None] != 0) | below) | same & below
    rank = jnp.cumsum(allowed.astype(jnp.int32), axis=1) - 1
    slots = jnp.arange(LIST, dtype=jnp.int32)
    chosen_slot = allowed[:, None, :] & (rank[:, None, :] == slots[None, :, None])
    listing = jnp.sum(jnp.where(chosen_slot, blocks[None, None, :] + 1, 0), axis=2) - 1
    return (segment, listing.astype(jnp.int32))


def draw_block_segment(key, part):
    return tree_layout(key)[0]


def draw_key_blocks(key, part):
    return tree_layout(key)[1]


def block_levels(rng, extent, pieces, smallest, top_value):
    factor_of, own = 1.0, jax.random.fold_in(rng, 6)
    for axis_at, blocks in pieces:
        steps = jnp.exp(jax.random.uniform(jax.random.fold_in(own, axis_at), (blocks,), jnp.float32, smallest / len(pieces), top_value / len(pieces)))
        factor_of = factor_of * jnp.repeat(steps, extent[axis_at] // blocks).reshape([-1 if axis == axis_at else 1 for axis in range(len(extent))])
    return factor_of


def gaussian(rng, dims, spread, reach, pieces=(), kind=jnp.bfloat16):
    values = spread * jax.random.normal(rng, dims, jnp.float32)
    if pieces:
        values = values * block_levels(rng, dims, pieces, -0.22, 0.18)
    return jnp.clip(values, -reach, reach).astype(kind)


def setup_inputs(seed: int = 0) -> dict:
    key_of = jax.random.split(jax.random.key(seed), 11)
    return {
        "hidden_in": draw_hidden_in(jax.random.fold_in(key_of[10], 71), 0),
        "norm_gain": jnp.clip(1.0 + 0.15 * jax.random.normal(key_of[1], (MODEL_WIDTH,), jnp.float32), 0.25, 1.75),
        "w_query": draw_w_query(jax.random.fold_in(key_of[10], 71), 0),
        "q_bias": gaussian(key_of[3], (QUERY_HEADS * HEAD_SIZE,), 0.5, 3.0, ((0, 2),)),
        "w_key": draw_w_key(jax.random.fold_in(key_of[10], 71), 0),
        "key_bias": gaussian(key_of[5], (KEY_VALUE_HEADS * HEAD_SIZE,), 0.5, 3.0, ((0, 2),)),
        "value_weight": gaussian(key_of[6], (MODEL_WIDTH, KEY_VALUE_HEADS * HEAD_SIZE), MODEL_WIDTH ** -0.5, 0.0625, ((0, 16), (1, 2))),
        "value_bias": gaussian(key_of[7], (KEY_VALUE_HEADS * HEAD_SIZE,), 0.3, 3.0, ((0, 2),)),
        "block_segment": draw_block_segment(jax.random.fold_in(key_of[10], 71), 0),
        "key_blocks": draw_key_blocks(jax.random.fold_in(key_of[10], 71), 0),
    }


ROPE_THETA = 1000000.0
EPSILON = 1e-06

def rms_norm(rows, gain):
    widened = rows.astype(jnp.float32)
    mean_square = lax.optimization_barrier(jnp.mean(widened * widened, axis=-1, keepdims=True))
    return (widened * lax.rsqrt(mean_square + EPSILON) * gain.astype(jnp.float32)).astype(jnp.bfloat16)

def apply_rotation(vectors, token_position):
    half = vectors.shape[-1] // 2
    frequencies = ROPE_THETA ** (-2.0 * jnp.arange(half, dtype=jnp.float32) / vectors.shape[-1])
    angles = token_position.astype(jnp.float32)[:, None] * frequencies[None, :]
    cosine = jnp.cos(angles)[:, None, :]
    sine = jnp.sin(angles)[:, None, :]
    former = vectors[..., :half]
    latter = vectors[..., half:]
    return jnp.concatenate([former * cosine - latter * sine, latter * cosine + former * sine], axis=-1)

def reference(hidden_in, norm_gain, w_query, q_bias, w_key, key_bias, value_weight, value_bias, block_segment, key_blocks):
    nblocks = TREE_TOKENS // BLK
    block_ids = jnp.arange(nblocks, dtype=jnp.int32)
    same = block_segment[:, None] == block_segment[None, :]
    leading = lax.optimization_barrier(jnp.min(jnp.where(same, block_ids[None, :], nblocks), axis=1)).astype(jnp.int32)
    tokens = jnp.arange(TREE_TOKENS, dtype=jnp.int32)
    blocks = (tokens // BLK).astype(jnp.int32)
    token_segment = block_segment[blocks]
    token_position = jnp.where(token_segment == 0, tokens, nblocks // 2 * BLK + tokens - leading[blocks] * BLK).astype(jnp.int32)
    normed = rms_norm(hidden_in, norm_gain)
    queries = jnp.dot(normed, w_query, preferred_element_type=jnp.float32) + q_bias.astype(jnp.float32)
    queries = apply_rotation(queries.reshape(TREE_TOKENS, QUERY_HEADS, HEAD_SIZE), token_position).astype(jnp.bfloat16)
    key_matrix = jnp.dot(normed, w_key, preferred_element_type=jnp.float32) + key_bias.astype(jnp.float32)
    key_matrix = apply_rotation(key_matrix.reshape(TREE_TOKENS, KEY_VALUE_HEADS, HEAD_SIZE), token_position).astype(jnp.bfloat16)
    value_matrix = (jnp.dot(normed, value_weight, preferred_element_type=jnp.float32) + value_bias.astype(jnp.float32)).astype(jnp.bfloat16)
    value_matrix = value_matrix.reshape(TREE_TOKENS, KEY_VALUE_HEADS, HEAD_SIZE)
    queries_wide = lax.optimization_barrier(queries).astype(jnp.float32)
    keys_wide = lax.optimization_barrier(key_matrix).astype(jnp.float32)
    values_wide = value_matrix.astype(jnp.float32)
    listed = jnp.any(key_blocks[:, :, None] == block_ids[None, None, :], axis=1)
    query_group = QUERY_HEADS // KEY_VALUE_HEADS
    rows = math.gcd(TREE_TOKENS, 512)
    scale = HEAD_SIZE ** (-0.5)

    def one_block(index):
        first = (index * rows).astype(jnp.int32)
        query_tok = first + jnp.arange(rows, dtype=jnp.int32)
        query_blk = (query_tok // BLK).astype(jnp.int32)
        query_seg = lax.dynamic_slice_in_dim(token_segment, first, rows, 0)
        allowed = listed[query_blk][:, blocks]
        causal = tokens[None, :] <= query_tok[:, None]
        visible = allowed & ((query_seg[:, None] != token_segment[None, :]) | causal)
        block_queries = lax.dynamic_slice_in_dim(queries_wide, first, rows, 0)

        def single_head(kv_head):
            head_queries = lax.dynamic_slice_in_dim(block_queries, (kv_head * query_group).astype(jnp.int32), query_group, 1)
            head_keys = lax.dynamic_index_in_dim(keys_wide, kv_head, 1, keepdims=False)
            head_values = lax.dynamic_index_in_dim(values_wide, kv_head, 1, keepdims=False)
            scores = jnp.einsum('qjd,kd->jqk', head_queries, head_keys) * scale
            masked = jnp.where(visible[None], scores, -jnp.inf)
            peak = lax.optimization_barrier(jnp.max(masked, axis=-1, keepdims=True))
            exponent = jnp.exp(masked - peak)
            total = lax.optimization_barrier(jnp.sum(exponent, axis=-1, keepdims=True))
            rounded = lax.optimization_barrier(exponent.astype(jnp.bfloat16)).astype(jnp.float32)
            return jnp.einsum('jqk,kd->jqd', rounded, head_values) / total
        head_stack = lax.map(single_head, jnp.arange(KEY_VALUE_HEADS, dtype=jnp.int32))
        return head_stack.transpose(2, 0, 1, 3).reshape(rows, QUERY_HEADS * HEAD_SIZE)
    out = lax.map(one_block, jnp.arange(TREE_TOKENS // rows, dtype=jnp.int32))
    return out.reshape(TREE_TOKENS, QUERY_HEADS * HEAD_SIZE).astype(jnp.bfloat16)
```

```python
import math

import jax
import jax.numpy as jnp
from jax import lax
from jax.experimental import pallas as pl
from jax.experimental.pallas import tpu as pltpu
from jax.sharding import PartitionSpec as P

HEAD_SIZE = 128
BLK = 128


ROPE_THETA = 1000000.0
EPSILON = 1e-06
NEG_FILL = -1e30


def rms_norm(rows, gain):
    widened = rows.astype(jnp.float32)
    mean_square = jnp.mean(widened * widened, axis=-1, keepdims=True)
    return (widened * lax.rsqrt(mean_square + EPSILON) * gain).astype(jnp.bfloat16)


def apply_rotation(vectors, token_position):
    half = vectors.shape[-1] // 2
    frequencies = ROPE_THETA ** (-2.0 * jnp.arange(half, dtype=jnp.float32) / vectors.shape[-1])
    angles = token_position.astype(jnp.float32)[:, None] * frequencies[None, :]
    cosine = jnp.cos(angles)[:, None, :]
    sine = jnp.sin(angles)[:, None, :]
    former = vectors[..., :half]
    latter = vectors[..., half:]
    return jnp.concatenate(
        [former * cosine - latter * sine, latter * cosine + former * sine], axis=-1
    )


def lookup(table, index):
    width = table.shape[0]
    hits = index[:, None] == jnp.arange(width, dtype=jnp.int32)[None, :]
    return jnp.sum(jnp.where(hits, table[None, :], 0), axis=1)


def token_facts(token_ids, block_segment):
    count = block_segment.shape[0]
    block_ids = jnp.arange(count, dtype=jnp.int32)
    same = block_segment[:, None] == block_segment[None, :]
    leading = jnp.min(jnp.where(same, block_ids[None, :], count), axis=1)
    blocks = token_ids // BLK
    segment = lookup(block_segment, blocks)
    token_position = jnp.where(
        segment == 0, token_ids, count // 2 * BLK + token_ids - lookup(leading, blocks) * BLK
    )
    return (token_position, segment)


def local(
    hidden_in,
    norm_gain,
    w_query,
    q_bias,
    w_key,
    key_bias,
    value_weight,
    value_bias,
    block_segment,
    key_blocks,
):
    rows_dev = hidden_in.shape[0]
    ctx_index = lax.axis_index("ctx")
    nblocks = block_segment.shape[0]
    heads_q = w_query.shape[1] // HEAD_SIZE
    heads_kv = w_key.shape[1] // HEAD_SIZE
    query_group = heads_q // heads_kv
    scale = HEAD_SIZE ** (-0.5)
    block_ids = jnp.arange(nblocks, dtype=jnp.int32)
    whole = lax.all_gather(hidden_in, "tp", axis=1, tiled=True)
    normed = rms_norm(whole, norm_gain)
    own_tokens = ctx_index * rows_dev + jnp.arange(rows_dev, dtype=jnp.int32)
    own_position, own_segment = token_facts(own_tokens, block_segment)
    listed = jnp.any(key_blocks[:, :, None] == block_ids[None, None, :], axis=1).astype(jnp.float32)

    def add_rows(piece):
        return jnp.dot(normed, piece, preferred_element_type=jnp.float32)

    key_total = add_rows(lax.all_gather(w_key, "ctx", axis=0, tiled=True))
    value_total = add_rows(lax.all_gather(value_weight, "ctx", axis=0, tiled=True))
    lifted = (key_total + key_bias.astype(jnp.float32)).reshape(rows_dev, heads_kv, HEAD_SIZE)
    key_matrix = (
        apply_rotation(lifted, own_position)
        .astype(jnp.bfloat16)
        .reshape(rows_dev, heads_kv * HEAD_SIZE)
    )
    value_matrix = (value_total + value_bias.astype(jnp.float32)).astype(jnp.bfloat16)
    key_matrix, value_matrix = (key_matrix, value_matrix)
    total = add_rows(lax.all_gather(w_query, "ctx", axis=0, tiled=True))
    lifted = (total + q_bias.astype(jnp.float32)).reshape(rows_dev, heads_q, HEAD_SIZE)
    queries = apply_rotation(lifted, own_position).astype(jnp.bfloat16)
    query_position, query_segment = token_facts(own_tokens, block_segment)
    query_onehot = ((own_tokens // BLK)[:, None] == block_ids[None, :]).astype(jnp.float32)
    query_listed = jnp.dot(query_onehot, listed, preferred_element_type=jnp.float32)
    arranged = (
        queries.reshape(rows_dev, heads_kv, query_group, HEAD_SIZE)
        .transpose(1, 2, 0, 3)
        .reshape(heads_kv, query_group * rows_dev, HEAD_SIZE)
    )
    initial = (
        jnp.full((heads_kv, query_group * rows_dev), NEG_FILL, jnp.float32),
        jnp.zeros((heads_kv, query_group * rows_dev), jnp.float32),
        jnp.zeros((heads_kv, query_group * rows_dev, HEAD_SIZE), jnp.float32),
    )

    def visit(state, key_tile, value_tile, tile_tokens):
        tile_blocks = tile_tokens // BLK
        tile_onehot = (tile_blocks[:, None] == block_ids[None, :]).astype(jnp.float32)
        in_list = jnp.dot(query_listed, tile_onehot.T, preferred_element_type=jnp.float32) > 0.5
        tile_segment = lookup(block_segment, tile_blocks)
        visible = in_list & (
            (query_segment[:, None] != tile_segment[None, :])
            | (tile_tokens[None, :] <= own_tokens[:, None])
        )

        def update(current):
            peak, denominator, accumulated = current
            scores = (
                jnp.einsum(
                    "gqd,kgd->gqk",
                    arranged,
                    key_tile.reshape(-1, heads_kv, HEAD_SIZE),
                    preferred_element_type=jnp.float32,
                )
                * scale
            )
            mask = jnp.tile(visible, (query_group, 1))[None]
            new_peak = jnp.maximum(peak, jnp.max(jnp.where(mask, scores, NEG_FILL), axis=-1))
            weights = jnp.where(mask, jnp.exp(scores - new_peak[..., None]), 0.0)
            factor = jnp.exp(peak - new_peak)
            denominator = denominator * factor + jnp.sum(weights, axis=-1)
            accumulated = accumulated * factor[..., None] + jnp.einsum(
                "gqk,kgd->gqd",
                weights.astype(jnp.bfloat16),
                value_tile.reshape(-1, heads_kv, HEAD_SIZE),
                preferred_element_type=jnp.float32,
            )
            return (new_peak, denominator, accumulated)

        def keep(current):
            return current

        return lax.cond(jnp.any(visible), update, keep, state)

    key_piece = lax.all_gather(key_matrix, "ctx", axis=0, tiled=True)
    value_piece = lax.all_gather(value_matrix, "ctx", axis=0, tiled=True)
    count = key_piece.shape[0]
    span = math.gcd(count, 512)
    steps = count // span

    def one_step(index, state):
        offset = index * span
        key_tile = lax.dynamic_slice_in_dim(key_piece, offset, span, 0)
        value_tile = lax.dynamic_slice_in_dim(value_piece, offset, span, 0)
        tile_tokens = 0 + offset + jnp.arange(span, dtype=jnp.int32)
        return visit(state, key_tile, value_tile, tile_tokens)

    final_state = lax.fori_loop(0, steps, one_step, initial)
    peak, denominator, accumulated = final_state
    attended = (accumulated / denominator[..., None]).reshape(
        heads_kv, query_group, rows_dev, HEAD_SIZE
    )
    attended = (
        attended.transpose(2, 0, 1, 3).reshape(rows_dev, heads_q * HEAD_SIZE).astype(jnp.bfloat16)
    )
    return attended


PLANES = 4
INNER = 4
TILE = 512
VMEM_BYTES = 60 << 20
GROUPS = ((0, 512), (512, 512))


def hold(value, *others):
    return lax.optimization_barrier((value,) + others)[0]


def fetch_weights(source, families, weight_buf, sems):
    copies = []
    depth = families[0].shape[0] // PLANES
    for f, family in enumerate(families):
        for z in range(PLANES):
            start = pl.multiple_of((z * INNER + source[f]) * depth, depth)
            copies.append(
                pltpu.make_async_copy(
                    family.at[pl.ds(z * depth, depth), :],
                    weight_buf.at[pl.ds(start, depth), :],
                    sems.at[f * PLANES + z],
                )
            )
    return copies


def rotate(part, turn_cos, turn_sin):
    return part * turn_cos + pltpu.roll(part, HEAD_SIZE // 2, 1) * turn_sin


def slot_kernel(
    flags, source, near, far, w0, w1, w2, w3, gain, bias, cosine, sine, out, kv, weight_buf, sems
):
    copies = fetch_weights(source, (w0, w1, w2, w3), weight_buf, sems)
    for copy in copies:
        copy.start()
    rows, half = near.shape
    step = 32
    mine = flags[0]

    def chunk(i, carry):
        at = pl.multiple_of(i * step, step)
        left = near[pl.ds(at, step), :].astype(jnp.float32)
        right = far[pl.ds(at, step), :].astype(jnp.float32)
        total = jnp.sum(left * left, axis=-1, keepdims=True) + jnp.sum(
            right * right, axis=-1, keepdims=True
        )
        factor = lax.rsqrt(total * (0.5 / half) + EPSILON)
        out[mine, pl.ds(at, step), :] = (left * factor * gain[pl.ds(mine, 1), :]).astype(
            jnp.bfloat16
        )
        out[1 - mine, pl.ds(at, step), :] = (right * factor * gain[pl.ds(1 - mine, 1), :]).astype(
            jnp.bfloat16
        )
        return carry

    lax.fori_loop(0, rows // step, chunk, 0)
    for copy in copies:
        copy.wait()
    total = jnp.dot(out[0], weight_buf[:half, :], preferred_element_type=jnp.float32) + jnp.dot(
        out[1], weight_buf[half:, :], preferred_element_type=jnp.float32
    )
    total = total + bias[...]
    start = pl.multiple_of(flags[1] * rows, rows)
    key = rotate(total[:, :HEAD_SIZE], cosine[pl.ds(start, rows), :], sine[pl.ds(start, rows), :])
    kv[:, :HEAD_SIZE] = key.astype(jnp.bfloat16)
    kv[:, HEAD_SIZE:] = total[:, HEAD_SIZE:].astype(jnp.bfloat16)


def do_slot(flags, source, near, far, families, gain, bias, cosine, sine):
    rows, half = near.shape
    columns = families[0].shape[1]
    in_vmem = pl.BlockSpec(memory_space=pltpu.VMEM)
    anywhere = pl.BlockSpec(memory_space=pl.ANY)
    scalars = pl.BlockSpec(memory_space=pltpu.SMEM)
    return pl.pallas_call(
        slot_kernel,
        out_shape=(
            jax.ShapeDtypeStruct((2, rows, half), jnp.bfloat16),
            jax.ShapeDtypeStruct((rows, columns), jnp.bfloat16),
        ),
        in_specs=[scalars, scalars, in_vmem, in_vmem] + [anywhere] * INNER + [in_vmem] * 4,
        out_specs=(in_vmem, in_vmem),
        scratch_shapes=[
            pltpu.VMEM((2 * half, columns), jnp.bfloat16),
            pltpu.SemaphoreType.DMA((4 * PLANES,)),
        ],
        compiler_params=pltpu.CompilerParams(vmem_limit_bytes=VMEM_BYTES),
        cost_estimate=pl.CostEstimate(
            flops=4 * rows * half * columns,
            transcendentals=0,
            bytes_accessed=8 * rows * half + 4 * half * columns,
        ),
        name="slot",
    )(flags, source, near, far, *families, gain, bias, cosine, sine)


def project_kernel(order, source, *refs):
    slots, families = refs[:PLANES], refs[PLANES : PLANES + INNER]
    bias, cosine, sine, out, rows_buf, weight_buf, total, row_sems, weight_sems = refs[PLANES + INNER :]
    rows, half = slots[0].shape[1:]
    columns = out.shape[1]
    depth = half * 2 // PLANES
    weight_copies = fetch_weights(source, families, weight_buf, weight_sems)
    waits = []
    for z in range(PLANES):
        part = (z * depth) // half
        within = z * depth - part * half
        chunk = [weight_copies[f * PLANES + z] for f in range(4)]
        for s in range(PLANES):
            chunk.append(
                pltpu.make_async_copy(
                    slots[s].at[part, :, pl.ds(within, depth)],
                    rows_buf.at[z, pl.ds(s * rows, rows), :],
                    row_sems.at[z * PLANES + s],
                )
            )
        for copy in chunk:
            copy.start()
        waits.append(chunk)
    for z in range(PLANES):
        for copy in waits[z]:
            copy.wait()
        product = jnp.dot(
            rows_buf[z],
            weight_buf[z * depth : (z + 1) * depth, :],
            preferred_element_type=jnp.float32,
        )
        if z == 0:
            total[...] = product
        elif z < PLANES - 1:
            total[...] += product
        else:
            total[...] = total[...] + product + bias[...]
    for s in range(PLANES):
        start = pl.multiple_of(order[s] * rows, rows)
        turn_cos = cosine[pl.ds(start, rows), :]
        turn_sin = sine[pl.ds(start, rows), :]
        for h in range(columns // HEAD_SIZE):
            part = total[s * rows : (s + 1) * rows, h * HEAD_SIZE : (h + 1) * HEAD_SIZE]
            out[pl.ds(start, rows), h * HEAD_SIZE : (h + 1) * HEAD_SIZE] = rotate(
                part, turn_cos, turn_sin
            ).astype(jnp.bfloat16)


def project(order, source, slots, families, bias, cosine, sine):
    rows, half = slots[0].shape[1:]
    columns = families[0].shape[1]
    in_vmem = pl.BlockSpec(memory_space=pltpu.VMEM)
    anywhere = pl.BlockSpec(memory_space=pl.ANY)
    scalars = pl.BlockSpec(memory_space=pltpu.SMEM)
    return pl.pallas_call(
        project_kernel,
        out_shape=jax.ShapeDtypeStruct((PLANES * rows, columns), jnp.bfloat16),
        in_specs=[scalars, scalars] + [anywhere] * (PLANES + INNER) + [in_vmem] * 3,
        out_specs=in_vmem,
        scratch_shapes=[
            pltpu.VMEM((PLANES, PLANES * rows, 2 * half // PLANES), jnp.bfloat16),
            pltpu.VMEM((2 * half, columns), jnp.bfloat16),
            pltpu.VMEM((PLANES * rows, columns), jnp.float32),
            pltpu.SemaphoreType.DMA((PLANES * PLANES,)),
            pltpu.SemaphoreType.DMA((4 * PLANES,)),
        ],
        compiler_params=pltpu.CompilerParams(vmem_limit_bytes=VMEM_BYTES),
        cost_estimate=pl.CostEstimate(
            flops=2 * PLANES * rows * 2 * half * columns,
            transcendentals=0,
            bytes_accessed=2 * (PLANES * rows * 2 * half + 2 * half * columns),
        ),
        name="project",
    )(order, source, *slots, *families, bias, cosine, sine)


def attend_kernel(total_rows, facts, places, queries, *refs):
    pieces = refs[:INNER]
    out, key_buf, value_buf, sems = refs[INNER:]
    at = pl.program_id(0)
    rows = pieces[0].shape[0] // PLANES
    heads = queries.shape[1] // HEAD_SIZE

    @pl.when(at == 0)
    def load():
        copies = []
        for p in range(INNER):
            for m in range(PLANES):
                start = pl.multiple_of(places[p * PLANES + m] * rows, rows)
                for part, buf in ((0, key_buf), (1, value_buf)):
                    copies.append(
                        pltpu.make_async_copy(
                            pieces[p].at[
                                pl.ds(m * rows, rows), pl.ds(part * HEAD_SIZE, HEAD_SIZE)
                            ],
                            buf.at[pl.ds(start, rows), pl.ds(0, HEAD_SIZE)],
                            sems.at[(p * PLANES + m) * 2 + part],
                        )
                    )
        for copy in copies:
            copy.start()
        extra = key_buf.shape[0] - total_rows
        key_buf[total_rows:, :] = jnp.zeros((extra, HEAD_SIZE), jnp.bfloat16)
        value_buf[total_rows:, :HEAD_SIZE] = jnp.zeros((extra, HEAD_SIZE), jnp.bfloat16)
        value_buf[:, HEAD_SIZE:] = jnp.ones((key_buf.shape[0], HEAD_SIZE), jnp.bfloat16)
        for copy in copies:
            copy.wait()

    per_step = queries.shape[0] // BLK
    count = pl.num_programs(0) * per_step
    full_tiles = facts[count + at * per_step]
    exponent = HEAD_SIZE ** (-0.5) * math.log2(math.e)
    chains = [(p, j) for p in range(per_step) for j in range(heads // 2)]

    def part(p, h):
        return (slice(p * BLK, (p + 1) * BLK), slice(h * HEAD_SIZE, (h + 1) * HEAD_SIZE))

    stacked = [
        jnp.concatenate([queries[part(p, 2 * j)], queries[part(p, 2 * j + 1)]], axis=0)
        for p, j in chains
    ]
    lines = 2 * BLK

    def update(state, number, keys, values, visible):
        peak, held = state
        scores = lax.dot_general(
            stacked[number], keys, (((1,), (1,)), ((), ())), preferred_element_type=jnp.float32
        )
        if visible is not None:
            scores = jnp.where(visible, scores, NEG_FILL)
        new_peak = jnp.maximum(peak, jnp.max(scores, axis=-1, keepdims=True))
        weights = jnp.exp2((scores - new_peak) * exponent)
        factor = jnp.exp2((peak - new_peak) * exponent)
        held = held * factor + jnp.dot(
            weights.astype(jnp.bfloat16), values, preferred_element_type=jnp.float32
        )
        return new_peak, held

    def whole_tile(t, state):
        start = pl.multiple_of(t * TILE, TILE)
        keys, values = key_buf[pl.ds(start, TILE), :], value_buf[pl.ds(start, TILE), :]
        return tuple(update(one, n, keys, values, None) for n, one in enumerate(state))

    state = tuple(
        (
            jnp.full((lines, 1), NEG_FILL, jnp.float32),
            jnp.zeros((lines, 2 * HEAD_SIZE), jnp.float32),
        )
        for _ in chains
    )
    state = lax.fori_loop(0, full_tiles, whole_tile, state)
    line = lax.broadcasted_iota(jnp.int32, (lines, TILE), 0) % BLK
    column = lax.broadcasted_iota(jnp.int32, (lines, TILE), 1)
    for number, (p, j) in enumerate(chains):
        block = facts[at * per_step + p]
        tail = pl.multiple_of(facts[2 * count + at * per_step + p] * BLK, BLK)
        keys, values = key_buf[pl.ds(tail, TILE), :], value_buf[pl.ds(tail, TILE), :]
        visible = column - line <= block * BLK - tail
        held = update(state[number], number, keys, values, visible)[1]
        done = (held[:, :HEAD_SIZE] / held[:, HEAD_SIZE:]).astype(jnp.bfloat16)
        out[part(p, 2 * j)] = done[:BLK]
        out[part(p, 2 * j + 1)] = done[BLK:]


def attend(facts, places, queries, pieces, total_rows):
    count, columns = queries.shape
    step = 2 * BLK

    def kernel(*refs):
        attend_kernel(total_rows, *refs)

    return pl.pallas_call(
        kernel,
        out_shape=jax.ShapeDtypeStruct((count, columns), jnp.bfloat16),
        grid_spec=pltpu.PrefetchScalarGridSpec(
            num_scalar_prefetch=2,
            grid=(count // step,),
            in_specs=[pl.BlockSpec((step, columns), lambda i, a, b: (i, 0))]
            + [pl.BlockSpec(memory_space=pl.ANY)] * INNER,
            out_specs=pl.BlockSpec((step, columns), lambda i, a, b: (i, 0)),
            scratch_shapes=[
                pltpu.VMEM((total_rows + TILE - BLK, HEAD_SIZE), jnp.bfloat16),
                pltpu.VMEM((total_rows + TILE - BLK, 2 * HEAD_SIZE), jnp.bfloat16),
                pltpu.SemaphoreType.DMA((INNER * PLANES * 2,)),
            ],
        ),
        compiler_params=pltpu.CompilerParams(vmem_limit_bytes=VMEM_BYTES),
        cost_estimate=pl.CostEstimate(
            flops=4 * count * columns * (total_rows // 2),
            transcendentals=count * (columns // HEAD_SIZE) * (total_rows // 2),
            bytes_accessed=4 * count * columns + 2 * total_rows * 2 * HEAD_SIZE,
        ),
        name="attend",
    )(facts, places, queries, *pieces)


def collect_kernel(*refs):
    pieces, out = refs[:-1], refs[-1]
    rows = out.shape[0]
    stride = out.shape[1] // PLANES
    offset = 0
    for piece in pieces:
        columns = piece.shape[1]
        for z in range(PLANES):
            start = z * stride + offset
            out[:, start : start + columns] = piece[z * rows : (z + 1) * rows, :]
        offset += columns


def collect(pieces, columns):
    in_vmem = pl.BlockSpec(memory_space=pltpu.VMEM)
    return pl.pallas_call(
        collect_kernel,
        out_shape=jax.ShapeDtypeStruct((pieces[0].shape[0] // PLANES, columns), jnp.bfloat16),
        in_specs=[in_vmem] * len(pieces),
        out_specs=in_vmem,
        name="collect",
    )(*pieces)


def by_planes(
    hidden_in,
    norm_gain,
    w_query,
    q_bias,
    w_key,
    key_bias,
    value_weight,
    value_bias,
    block_segment,
    key_blocks,
):
    devices = PLANES * INNER
    ctx_index = lax.axis_index("ctx").astype(jnp.int32)
    tp_index = lax.axis_index("tp").astype(jnp.int32)
    plane = ctx_index // INNER
    inner = ctx_index % INNER
    rows, half = hidden_in.shape
    nblocks = block_segment.shape[0]
    head_columns = w_query.shape[1] // PLANES

    def swap(array, bits):
        return lax.ppermute(array, "ctx", [(i, i ^ bits) for i in range(devices)])

    def pair_planes(array, low):
        def partner(i):
            z = i // INNER
            to = low + ((z - low) ^ 1)
            return i + (to - z) * INNER if low <= z and 0 <= to < PLANES else i

        return lax.ppermute(array, "ctx", [(i, partner(i)) for i in range(devices)])

    def across(array):
        return lax.ppermute(array, "tp", [(0, 1), (1, 0)])

    def exchange(array):
        return lax.all_to_all(
            array,
            "ctx",
            0,
            0,
            axis_index_groups=[
                [z * INNER + r for z in range(PLANES)] for r in range(INNER)
            ],
            tiled=True,
        )

    def stacked_columns(array, stride, offset, columns):
        return [
            lax.slice_in_dim(array, z * stride + offset, z * stride + offset + columns, axis=1)
            for z in range(PLANES)
        ]

    kv_send = jnp.concatenate(
        [
            jnp.concatenate(pair, axis=1)
            for pair in zip(
                stacked_columns(w_key, HEAD_SIZE, 0, HEAD_SIZE),
                stacked_columns(value_weight, HEAD_SIZE, 0, HEAD_SIZE),
            )
        ],
        axis=0,
    )
    query_send = [
        jnp.concatenate(stacked_columns(w_query, head_columns, offset, columns), axis=0)
        for offset, columns in GROUPS
    ]
    table = jnp.asarray([[0, 1, 2, 3], [1, 0, 2, 3], [2, 3, 1, 0], [3, 2, 1, 0]], jnp.int32)
    order = lax.dynamic_index_in_dim(table, plane, 0, keepdims=False)
    bits = jnp.asarray([0, 2, 1, 3], jnp.int32)
    source = inner ^ bits

    each = jnp.arange(PLANES, dtype=jnp.int32)
    tokens = (
        (each * (INNER * rows) + inner * rows)[:, None]
        + jnp.arange(rows, dtype=jnp.int32)[None, :]
    ).reshape(-1)
    position, _ = token_facts(tokens, block_segment)
    frequencies = ROPE_THETA ** (
        -2.0 * jnp.arange(HEAD_SIZE // 2, dtype=jnp.float32) / HEAD_SIZE
    )
    angles = position.astype(jnp.float32)[:, None] * frequencies[None, :]
    cosine, sine = jnp.cos(angles), jnp.sin(angles)
    cosine = jnp.concatenate([cosine, cosine], axis=1)
    sine = jnp.concatenate([-sine, sine], axis=1)

    gain = norm_gain.reshape(2, half)
    kv_bias = jnp.concatenate(
        [
            lax.dynamic_slice_in_dim(key_bias, plane * HEAD_SIZE, HEAD_SIZE, 0),
            lax.dynamic_slice_in_dim(value_bias, plane * HEAD_SIZE, HEAD_SIZE, 0),
        ]
    ).astype(jnp.float32)[None]
    def slot(number, near, far):
        flags = jnp.stack([tp_index, order[number]])
        return do_slot(flags, source, near, far, kv_families, gain, kv_bias, cosine, sine)

    inside = (plane != 0) & (plane != PLANES - 1)
    phase = lax.optimization_barrier
    near1, swap_in = pair_planes(hidden_in, 0), pair_planes(hidden_in, 1)
    far0 = across(hidden_in)
    near1, swap_in, far0, kv_send, cosine, sine, *query_send = phase(
        (near1, swap_in, far0, kv_send, cosine, sine, *query_send)
    )

    swap_2a, swap_2b = pair_planes(swap_in, 0), pair_planes(near1, 1)
    far1 = across(near1)
    kv_a = exchange(kv_send)
    swap_in, swap_2a, swap_2b, far1, kv_a, *query_send = phase(
        (swap_in, swap_2a, swap_2b, far1, kv_a, *query_send)
    )

    swap_3 = pair_planes(swap_2b, 0)
    near2 = jnp.where(inside, swap_in, swap_2a)
    far2 = across(near2)
    kv_b, kv_c = swap(kv_a, 2), swap(kv_a, 1)
    kv_d = swap(kv_b, 1)
    qa_a = exchange(query_send[0])
    swap_2b, swap_3, near2, far2, kv_b, kv_c, kv_d, qa_a, *query_send = phase(
        (swap_2b, swap_3, near2, far2, kv_b, kv_c, kv_d, qa_a, *query_send)
    )

    kv_families = (kv_a, kv_b, kv_c, kv_d)
    near3 = jnp.where(inside, swap_2b, swap_3)
    far3 = across(near3)
    qa_b, qa_c = swap(qa_a, 2), swap(qa_a, 1)
    qa_d = swap(qa_b, 1)
    qb_a = exchange(query_send[1])
    early = [slot(0, hidden_in, far0), slot(1, near1, far1), slot(2, near2, far2)]
    far3, near3, qa_b, qa_c, qa_d, qb_a, early = phase(
        (far3, near3, qa_b, qa_c, qa_d, qb_a, early)
    )

    qb_b, qb_c = swap(qb_a, 2), swap(qb_a, 1)
    slots, key_value = zip(*early, slot(3, near3, far3))
    key_value = jnp.concatenate(key_value, axis=0)
    kv_all = [key_value, swap(key_value, 2), swap(key_value, 1), swap(key_value, 3)]
    places = (order[None, :] * INNER + source[:, None]).reshape(-1)

    per_rows = rows // BLK
    blocks = (
        (each * INNER + inner)[:, None] * per_rows
        + jnp.arange(per_rows, dtype=jnp.int32)[None, :]
    ).reshape(-1)
    block_ids = jnp.arange(nblocks, dtype=jnp.int32)
    same = block_segment[:, None] == block_segment[None, :]
    leading = jnp.min(jnp.where(same, block_ids[None, :], nblocks), axis=1).astype(jnp.int32)
    prompt = blocks < nblocks // 2
    per_tile = TILE // BLK
    full_tiles = jnp.where(prompt, blocks // per_tile, nblocks // 2 // per_tile)
    tail = jnp.where(prompt, blocks // per_tile * per_tile, lookup(leading, blocks))
    facts = jnp.concatenate([blocks, full_tiles, tail]).astype(jnp.int32)

    def queries_of(group, families):
        offset, columns = GROUPS[group]
        bias = lax.dynamic_slice_in_dim(q_bias, plane * head_columns + offset, columns, 0)
        return project(
            order, source, slots, families, bias.astype(jnp.float32)[None], cosine, sine
        )

    def attended_by(queries):
        return attend(facts, places, queries, kv_all, nblocks * BLK)

    attended_a = attended_by(queries_of(0, (qa_a, qa_b, qa_c, qa_d)))
    qb_b, qb_c, attended_a = phase((qb_b, qb_c, attended_a))
    qb_d = swap(qb_b, 1)
    finished_a = exchange(attended_a)
    attended_b = attended_by(queries_of(1, (qb_a, qb_b, qb_c, qb_d)))
    return collect([finished_a, exchange(attended_b)], w_query.shape[1])


def solution(mesh):
    placed = (
        P("ctx", "tp"),
        P(),
        P("ctx", "tp"),
        P("tp"),
        P("ctx", "tp"),
        P("tp"),
        P("ctx", "tp"),
        P("tp"),
        P(),
        P(),
    )
    planes = mesh.shape["ctx"] == PLANES * INNER and mesh.shape["tp"] == 2
    return jax.shard_map(
        by_planes if planes else local,
        mesh=mesh,
        in_specs=placed,
        out_specs=P("ctx", "tp"),
        check_vma=False,
    )
```

```python
import math

import jax
import jax.numpy as jnp
from jax import lax
from jax.experimental import pallas as pl
from jax.experimental.pallas import tpu as pltpu
from jax.sharding import PartitionSpec as P

HEAD_SIZE = 128
BLK = 128


ROPE_THETA = 1000000.0
EPSILON = 1e-06
NEG_FILL = -1e30


def rms_norm(rows, gain):
    widened = rows.astype(jnp.float32)
    mean_square = jnp.mean(widened * widened, axis=-1, keepdims=True)
    return (widened * lax.rsqrt(mean_square + EPSILON) * gain).astype(jnp.bfloat16)


def apply_rotation(vectors, token_position):
    half = vectors.shape[-1] // 2
    frequencies = ROPE_THETA ** (-2.0 * jnp.arange(half, dtype=jnp.float32) / vectors.shape[-1])
    angles = token_position.astype(jnp.float32)[:, None] * frequencies[None, :]
    cosine = jnp.cos(angles)[:, None, :]
    sine = jnp.sin(angles)[:, None, :]
    former = vectors[..., :half]
    latter = vectors[..., half:]
    return jnp.concatenate(
        [former * cosine - latter * sine, latter * cosine + former * sine], axis=-1
    )


def lookup(table, index):
    width = table.shape[0]
    hits = index[:, None] == jnp.arange(width, dtype=jnp.int32)[None, :]
    return jnp.sum(jnp.where(hits, table[None, :], 0), axis=1)


def token_facts(token_ids, block_segment):
    count = block_segment.shape[0]
    block_ids = jnp.arange(count, dtype=jnp.int32)
    same = block_segment[:, None] == block_segment[None, :]
    leading = jnp.min(jnp.where(same, block_ids[None, :], count), axis=1)
    blocks = token_ids // BLK
    segment = lookup(block_segment, blocks)
    token_position = jnp.where(
        segment == 0, token_ids, count // 2 * BLK + token_ids - lookup(leading, blocks) * BLK
    )
    return (token_position, segment)


def local(
    hidden_in,
    norm_gain,
    w_query,
    q_bias,
    w_key,
    key_bias,
    value_weight,
    value_bias,
    block_segment,
    key_blocks,
):
    rows_dev = hidden_in.shape[0]
    ctx_index = lax.axis_index("ctx")
    nblocks = block_segment.shape[0]
    heads_q = w_query.shape[1] // HEAD_SIZE
    heads_kv = w_key.shape[1] // HEAD_SIZE
    query_group = heads_q // heads_kv
    scale = HEAD_SIZE ** (-0.5)
    block_ids = jnp.arange(nblocks, dtype=jnp.int32)
    whole = lax.all_gather(hidden_in, "tp", axis=1, tiled=True)
    normed = rms_norm(whole, norm_gain)
    own_tokens = ctx_index * rows_dev + jnp.arange(rows_dev, dtype=jnp.int32)
    own_position, own_segment = token_facts(own_tokens, block_segment)
    listed = jnp.any(key_blocks[:, :, None] == block_ids[None, None, :], axis=1).astype(jnp.float32)

    def add_rows(piece):
        return jnp.dot(normed, piece, preferred_element_type=jnp.float32)

    key_total = add_rows(lax.all_gather(w_key, "ctx", axis=0, tiled=True))
    value_total = add_rows(lax.all_gather(value_weight, "ctx", axis=0, tiled=True))
    lifted = (key_total + key_bias.astype(jnp.float32)).reshape(rows_dev, heads_kv, HEAD_SIZE)
    key_matrix = (
        apply_rotation(lifted, own_position)
        .astype(jnp.bfloat16)
        .reshape(rows_dev, heads_kv * HEAD_SIZE)
    )
    value_matrix = (value_total + value_bias.astype(jnp.float32)).astype(jnp.bfloat16)
    key_matrix, value_matrix = (key_matrix, value_matrix)
    total = add_rows(lax.all_gather(w_query, "ctx", axis=0, tiled=True))
    lifted = (total + q_bias.astype(jnp.float32)).reshape(rows_dev, heads_q, HEAD_SIZE)
    queries = apply_rotation(lifted, own_position).astype(jnp.bfloat16)
    query_position, query_segment = token_facts(own_tokens, block_segment)
    query_onehot = ((own_tokens // BLK)[:, None] == block_ids[None, :]).astype(jnp.float32)
    query_listed = jnp.dot(query_onehot, listed, preferred_element_type=jnp.float32)
    arranged = (
        queries.reshape(rows_dev, heads_kv, query_group, HEAD_SIZE)
        .transpose(1, 2, 0, 3)
        .reshape(heads_kv, query_group * rows_dev, HEAD_SIZE)
    )
    initial = (
        jnp.full((heads_kv, query_group * rows_dev), NEG_FILL, jnp.float32),
        jnp.zeros((heads_kv, query_group * rows_dev), jnp.float32),
        jnp.zeros((heads_kv, query_group * rows_dev, HEAD_SIZE), jnp.float32),
    )

    def visit(state, key_tile, value_tile, tile_tokens):
        tile_blocks = tile_tokens // BLK
        tile_onehot = (tile_blocks[:, None] == block_ids[None, :]).astype(jnp.float32)
        in_list = jnp.dot(query_listed, tile_onehot.T, preferred_element_type=jnp.float32) > 0.5
        tile_segment = lookup(block_segment, tile_blocks)
        visible = in_list & (
            (query_segment[:, None] != tile_segment[None, :])
            | (tile_tokens[None, :] <= own_tokens[:, None])
        )

        def update(current):
            peak, denominator, accumulated = current
            scores = (
                jnp.einsum(
                    "gqd,kgd->gqk",
                    arranged,
                    key_tile.reshape(-1, heads_kv, HEAD_SIZE),
                    preferred_element_type=jnp.float32,
                )
                * scale
            )
            mask = jnp.tile(visible, (query_group, 1))[None]
            new_peak = jnp.maximum(peak, jnp.max(jnp.where(mask, scores, NEG_FILL), axis=-1))
            weights = jnp.where(mask, jnp.exp(scores - new_peak[..., None]), 0.0)
            factor = jnp.exp(peak - new_peak)
            denominator = denominator * factor + jnp.sum(weights, axis=-1)
            accumulated = accumulated * factor[..., None] + jnp.einsum(
                "gqk,kgd->gqd",
                weights.astype(jnp.bfloat16),
                value_tile.reshape(-1, heads_kv, HEAD_SIZE),
                preferred_element_type=jnp.float32,
            )
            return (new_peak, denominator, accumulated)

        def keep(current):
            return current

        return lax.cond(jnp.any(visible), update, keep, state)

    key_piece = lax.all_gather(key_matrix, "ctx", axis=0, tiled=True)
    value_piece = lax.all_gather(value_matrix, "ctx", axis=0, tiled=True)
    count = key_piece.shape[0]
    span = math.gcd(count, 512)
    steps = count // span

    def one_step(index, state):
        offset = index * span
        key_tile = lax.dynamic_slice_in_dim(key_piece, offset, span, 0)
        value_tile = lax.dynamic_slice_in_dim(value_piece, offset, span, 0)
        tile_tokens = 0 + offset + jnp.arange(span, dtype=jnp.int32)
        return visit(state, key_tile, value_tile, tile_tokens)

    final_state = lax.fori_loop(0, steps, one_step, initial)
    peak, denominator, accumulated = final_state
    attended = (accumulated / denominator[..., None]).reshape(
        heads_kv, query_group, rows_dev, HEAD_SIZE
    )
    attended = (
        attended.transpose(2, 0, 1, 3).reshape(rows_dev, heads_q * HEAD_SIZE).astype(jnp.bfloat16)
    )
    return attended


PLANES = 4
INNER = 4
TILE = 512
VMEM_BYTES = 60 << 20
COLUMNS = 256


def hold(value, *others):
    return lax.optimization_barrier((value,) + others)[0]


def fetch_weights(source, families, weight_buf, sems):
    depth = families[0].shape[0] // PLANES
    copies = [[] for _ in range(PLANES)]
    for f, family in enumerate(families):
        columns = family.shape[1]
        first = f // INNER * columns
        for z in range(PLANES):
            start = pl.multiple_of((z * INNER + source[f % INNER]) * depth, depth)
            copies[z].append(
                pltpu.make_async_copy(
                    family.at[pl.ds(z * depth, depth), :],
                    weight_buf.at[pl.ds(start, depth), pl.ds(first, columns)],
                    sems.at[f * PLANES + z],
                )
            )
    return copies


def rotate(part, turn_cos, turn_sin):
    return part * turn_cos + pltpu.roll(part, HEAD_SIZE // 2, 1) * turn_sin


def slot_kernel(
    flags, source, near, far, w0, w1, w2, w3, gain, bias, cosine, sine, out, kv, weight_buf, sems
):
    copies = sum(fetch_weights(source, (w0, w1, w2, w3), weight_buf, sems), [])
    for copy in copies:
        copy.start()
    rows, half = near.shape
    step = 32
    mine = flags[0]

    def chunk(i, carry):
        at = pl.multiple_of(i * step, step)
        left = near[pl.ds(at, step), :].astype(jnp.float32)
        right = far[pl.ds(at, step), :].astype(jnp.float32)
        total = jnp.sum(left * left, axis=-1, keepdims=True) + jnp.sum(
            right * right, axis=-1, keepdims=True
        )
        factor = lax.rsqrt(total * (0.5 / half) + EPSILON)
        out[mine, pl.ds(at, step), :] = (left * factor * gain[pl.ds(mine, 1), :]).astype(
            jnp.bfloat16
        )
        out[1 - mine, pl.ds(at, step), :] = (right * factor * gain[pl.ds(1 - mine, 1), :]).astype(
            jnp.bfloat16
        )
        return carry

    lax.fori_loop(0, rows // step, chunk, 0)
    for copy in copies:
        copy.wait()
    total = jnp.dot(out[0], weight_buf[:half, :], preferred_element_type=jnp.float32) + jnp.dot(
        out[1], weight_buf[half:, :], preferred_element_type=jnp.float32
    )
    total = total + bias[...]
    start = pl.multiple_of(flags[1] * rows, rows)
    key = rotate(total[:, :HEAD_SIZE], cosine[pl.ds(start, rows), :], sine[pl.ds(start, rows), :])
    kv[:, :HEAD_SIZE] = key.astype(jnp.bfloat16)
    kv[:, HEAD_SIZE:] = total[:, HEAD_SIZE:].astype(jnp.bfloat16)


def do_slot(flags, source, near, far, families, gain, bias, cosine, sine):
    rows, half = near.shape
    columns = families[0].shape[1]
    in_vmem = pl.BlockSpec(memory_space=pltpu.VMEM)
    anywhere = pl.BlockSpec(memory_space=pl.ANY)
    scalars = pl.BlockSpec(memory_space=pltpu.SMEM)
    return pl.pallas_call(
        slot_kernel,
        out_shape=(
            jax.ShapeDtypeStruct((2, rows, half), jnp.bfloat16),
            jax.ShapeDtypeStruct((rows, columns), jnp.bfloat16),
        ),
        in_specs=[scalars, scalars, in_vmem, in_vmem] + [anywhere] * INNER + [in_vmem] * 4,
        out_specs=(in_vmem, in_vmem),
        scratch_shapes=[
            pltpu.VMEM((2 * half, columns), jnp.bfloat16),
            pltpu.SemaphoreType.DMA((4 * PLANES,)),
        ],
        compiler_params=pltpu.CompilerParams(vmem_limit_bytes=VMEM_BYTES),
        cost_estimate=pl.CostEstimate(
            flops=4 * rows * half * columns,
            transcendentals=0,
            bytes_accessed=8 * rows * half + 4 * half * columns,
        ),
        name="slot",
    )(flags, source, near, far, *families, gain, bias, cosine, sine)


def project_kernel(order, source, *refs):
    slots, families = refs[:PLANES], refs[PLANES:-9]
    bias, cosine, sine, out, rows_buf, weight_buf, total, row_sems, weight_sems = refs[-9:]
    rows, half = slots[0].shape[1:]
    columns = out.shape[1]
    depth = half * 2 // PLANES
    chunks = fetch_weights(source, families, weight_buf, weight_sems)
    for z, chunk in enumerate(chunks):
        part = (z * depth) // half
        within = z * depth - part * half
        for s in range(PLANES):
            chunk.append(
                pltpu.make_async_copy(
                    slots[s].at[part, :, pl.ds(within, depth)],
                    rows_buf.at[z, pl.ds(s * rows, rows), :],
                    row_sems.at[z * PLANES + s],
                )
            )
        for copy in chunk:
            copy.start()
    for z, chunk in enumerate(chunks):
        for copy in chunk:
            copy.wait()
        product = jnp.dot(
            rows_buf[z],
            weight_buf[z * depth : (z + 1) * depth, :],
            preferred_element_type=jnp.float32,
        )
        if z == 0:
            total[...] = product
        elif z < PLANES - 1:
            total[...] += product
        else:
            total[...] = total[...] + product + bias[...]
    for s in range(PLANES):
        start = pl.multiple_of(order[s] * rows, rows)
        turn_cos = cosine[pl.ds(start, rows), :]
        turn_sin = sine[pl.ds(start, rows), :]
        for h in range(columns // HEAD_SIZE):
            part = total[s * rows : (s + 1) * rows, h * HEAD_SIZE : (h + 1) * HEAD_SIZE]
            out[pl.ds(start, rows), h * HEAD_SIZE : (h + 1) * HEAD_SIZE] = rotate(
                part, turn_cos, turn_sin
            ).astype(jnp.bfloat16)


def project(order, source, slots, families, bias, cosine, sine):
    rows, half = slots[0].shape[1:]
    columns = families[0].shape[1] * (len(families) // INNER)
    in_vmem = pl.BlockSpec(memory_space=pltpu.VMEM)
    anywhere = pl.BlockSpec(memory_space=pl.ANY)
    scalars = pl.BlockSpec(memory_space=pltpu.SMEM)
    return pl.pallas_call(
        project_kernel,
        out_shape=jax.ShapeDtypeStruct((PLANES * rows, columns), jnp.bfloat16),
        in_specs=[scalars, scalars] + [anywhere] * (PLANES + len(families)) + [in_vmem] * 3,
        out_specs=in_vmem,
        scratch_shapes=[
            pltpu.VMEM((PLANES, PLANES * rows, 2 * half // PLANES), jnp.bfloat16),
            pltpu.VMEM((2 * half, columns), jnp.bfloat16),
            pltpu.VMEM((PLANES * rows, columns), jnp.float32),
            pltpu.SemaphoreType.DMA((PLANES * PLANES,)),
            pltpu.SemaphoreType.DMA((len(families) * PLANES,)),
        ],
        compiler_params=pltpu.CompilerParams(vmem_limit_bytes=VMEM_BYTES),
        cost_estimate=pl.CostEstimate(
            flops=2 * PLANES * rows * 2 * half * columns,
            transcendentals=0,
            bytes_accessed=2 * (PLANES * rows * 2 * half + 2 * half * columns),
        ),
        name="project",
    )(order, source, *slots, *families, bias, cosine, sine)


def attend_kernel(total_rows, facts, places, chunks, queries, *refs):
    pieces = refs[: 2 * INNER]
    out, key_buf, value_buf, sems = refs[2 * INNER :]
    at = pl.program_id(0)
    rows = pieces[-1].shape[0]
    heads = queries.shape[1] // HEAD_SIZE

    @pl.when(at == 0)
    def load():
        copies = []
        for p in range(INNER):
            for m in range(PLANES):
                start = pl.multiple_of(places[p * PLANES + m] * rows, rows)
                late = m == PLANES - 1
                for part, buf in ((0, key_buf), (1, value_buf)):
                    copies.append(
                        pltpu.make_async_copy(
                            pieces[p + INNER if late else p].at[
                                pl.ds(0 if late else m * rows, rows),
                                pl.ds(part * HEAD_SIZE, HEAD_SIZE),
                            ],
                            buf.at[pl.ds(start, rows), pl.ds(0, HEAD_SIZE)],
                            sems.at[(p * PLANES + m) * 2 + part],
                        )
                    )
        for copy in copies:
            copy.start()
        extra = key_buf.shape[0] - total_rows
        key_buf[total_rows:, :] = jnp.zeros((extra, HEAD_SIZE), jnp.bfloat16)
        value_buf[total_rows:, :HEAD_SIZE] = jnp.zeros((extra, HEAD_SIZE), jnp.bfloat16)
        value_buf[:, HEAD_SIZE:] = jnp.ones((key_buf.shape[0], HEAD_SIZE), jnp.bfloat16)
        for copy in copies:
            copy.wait()

    per_step = queries.shape[0] // BLK
    count = total_rows // INNER // BLK
    first_block = chunks[at] * per_step
    full_tiles = facts[count + first_block]
    exponent = HEAD_SIZE ** (-0.5) * math.log2(math.e)
    chains = [(p, j) for p in range(per_step) for j in range(heads // 2)]

    def part(p, h):
        return (slice(p * BLK, (p + 1) * BLK), slice(h * HEAD_SIZE, (h + 1) * HEAD_SIZE))

    stacked = [
        jnp.concatenate([queries[part(p, 2 * j)], queries[part(p, 2 * j + 1)]], axis=0)
        for p, j in chains
    ]
    lines = 2 * BLK

    def update(state, number, keys, values, visible):
        peak, held = state
        scores = lax.dot_general(
            stacked[number], keys, (((1,), (1,)), ((), ())), preferred_element_type=jnp.float32
        )
        if visible is not None:
            scores = jnp.where(visible, scores, NEG_FILL)
        new_peak = jnp.maximum(peak, jnp.max(scores, axis=-1, keepdims=True))
        weights = jnp.exp2((scores - new_peak) * exponent)
        factor = jnp.exp2((peak - new_peak) * exponent)
        held = held * factor + jnp.dot(
            weights.astype(jnp.bfloat16), values, preferred_element_type=jnp.float32
        )
        return new_peak, held

    def tiles(start, size, state):
        keys, values = key_buf[pl.ds(start, size), :], value_buf[pl.ds(start, size), :]
        return tuple(update(one, n, keys, values, None) for n, one in enumerate(state))

    def double_tile(t, state):
        return tiles(pl.multiple_of(t * 2 * TILE, 2 * TILE), 2 * TILE, state)

    def odd_tile(t, state):
        return tiles(pl.multiple_of((full_tiles - 1) * TILE, TILE), TILE, state)

    state = tuple(
        (
            jnp.full((lines, 1), NEG_FILL, jnp.float32),
            jnp.zeros((lines, 2 * HEAD_SIZE), jnp.float32),
        )
        for _ in chains
    )
    state = lax.fori_loop(0, full_tiles // 2, double_tile, state)
    state = lax.fori_loop(0, full_tiles % 2, odd_tile, state)
    line = lax.broadcasted_iota(jnp.int32, (lines, TILE), 0) % BLK
    column = lax.broadcasted_iota(jnp.int32, (lines, TILE), 1)
    for number, (p, j) in enumerate(chains):
        block = facts[first_block + p]
        tail = pl.multiple_of(facts[2 * count + first_block + p] * BLK, BLK)
        keys, values = key_buf[pl.ds(tail, TILE), :], value_buf[pl.ds(tail, TILE), :]
        visible = column - line <= block * BLK - tail
        held = update(state[number], number, keys, values, visible)[1]
        done = (held[:, :HEAD_SIZE] / held[:, HEAD_SIZE:]).astype(jnp.bfloat16)
        out[part(p, 2 * j)] = done[:BLK]
        out[part(p, 2 * j + 1)] = done[BLK:]


def attend(facts, places, chunks, queries, pieces, total_rows):
    columns = queries.shape[1]
    step = queries.shape[0] // PLANES
    count = chunks.shape[0] * step

    def kernel(*refs):
        attend_kernel(total_rows, *refs)

    return pl.pallas_call(
        kernel,
        out_shape=jax.ShapeDtypeStruct((count, columns), jnp.bfloat16),
        grid_spec=pltpu.PrefetchScalarGridSpec(
            num_scalar_prefetch=3,
            grid=(chunks.shape[0],),
            in_specs=[pl.BlockSpec((step, columns), lambda i, a, b, c: (c[i], 0))]
            + [pl.BlockSpec(memory_space=pl.ANY)] * (2 * INNER),
            out_specs=pl.BlockSpec((step, columns), lambda i, a, b, c: (i, 0)),
            scratch_shapes=[
                pltpu.VMEM((total_rows + TILE - BLK, HEAD_SIZE), jnp.bfloat16),
                pltpu.VMEM((total_rows + TILE - BLK, 2 * HEAD_SIZE), jnp.bfloat16),
                pltpu.SemaphoreType.DMA((INNER * PLANES * 2,)),
            ],
        ),
        compiler_params=pltpu.CompilerParams(vmem_limit_bytes=VMEM_BYTES),
        cost_estimate=pl.CostEstimate(
            flops=4 * count * columns * (total_rows // 2),
            transcendentals=count * (columns // HEAD_SIZE) * (total_rows // 2),
            bytes_accessed=4 * count * columns + 2 * total_rows * 2 * HEAD_SIZE,
        ),
        name="attend",
    )(facts, places, chunks, queries, *pieces)


def collect_kernel(places, *refs):
    pieces, out = refs[:-1], refs[-1]
    for k, piece in enumerate(pieces):
        start = pl.multiple_of(places[k], HEAD_SIZE)
        out[:, pl.ds(start, piece.shape[1])] = piece[...]


def collect(places, pieces, columns):
    in_vmem = pl.BlockSpec(memory_space=pltpu.VMEM)
    return pl.pallas_call(
        collect_kernel,
        out_shape=jax.ShapeDtypeStruct((pieces[0].shape[0], columns), jnp.bfloat16),
        in_specs=[pl.BlockSpec(memory_space=pltpu.SMEM)] + [in_vmem] * len(pieces),
        out_specs=in_vmem,
        name="collect",
    )(places, *pieces)


def by_planes(
    hidden_in,
    norm_gain,
    w_query,
    q_bias,
    w_key,
    key_bias,
    value_weight,
    value_bias,
    block_segment,
    key_blocks,
):
    devices = PLANES * INNER
    ctx_index = lax.axis_index("ctx").astype(jnp.int32)
    tp_index = lax.axis_index("tp").astype(jnp.int32)
    plane = ctx_index // INNER
    inner = ctx_index % INNER
    rows, half = hidden_in.shape
    nblocks = block_segment.shape[0]
    head_columns = w_query.shape[1] // PLANES

    def swap(array, bits):
        return lax.ppermute(array, "ctx", [(i, i ^ bits) for i in range(devices)])

    def pair_planes(array, low):
        def partner(i):
            z = i // INNER
            to = low + ((z - low) ^ 1)
            return i + (to - z) * INNER if low <= z and 0 <= to < PLANES else i

        return lax.ppermute(array, "ctx", [(i, partner(i)) for i in range(devices)])

    def across(array):
        return lax.ppermute(array, "tp", [(0, 1), (1, 0)])

    def exchange(array):
        return lax.all_to_all(
            array,
            "ctx",
            0,
            0,
            axis_index_groups=[
                [z * INNER + r for z in range(PLANES)] for r in range(INNER)
            ],
            tiled=True,
        )

    def stacked_columns(array, stride, offset, columns):
        return [
            lax.slice_in_dim(array, z * stride + offset, z * stride + offset + columns, axis=1)
            for z in range(PLANES)
        ]

    kv_send = jnp.concatenate(
        [
            jnp.concatenate(pair, axis=1)
            for pair in zip(
                stacked_columns(w_key, HEAD_SIZE, 0, HEAD_SIZE),
                stacked_columns(value_weight, HEAD_SIZE, 0, HEAD_SIZE),
            )
        ],
        axis=0,
    )
    query_send = [
        jnp.concatenate(stacked_columns(w_query, head_columns, offset, COLUMNS), axis=0)
        for offset in range(0, head_columns, COLUMNS)
    ]
    table = jnp.asarray([[0, 1, 2, 3], [1, 0, 2, 3], [2, 3, 1, 0], [3, 2, 1, 0]], jnp.int32)
    order = lax.dynamic_index_in_dim(table, plane, 0, keepdims=False)
    bits = jnp.asarray([0, 2, 1, 3], jnp.int32)
    source = inner ^ bits

    each = jnp.arange(PLANES, dtype=jnp.int32)
    tokens = (
        (each * (INNER * rows) + inner * rows)[:, None]
        + jnp.arange(rows, dtype=jnp.int32)[None, :]
    ).reshape(-1)
    position, _ = token_facts(tokens, block_segment)
    frequencies = ROPE_THETA ** (
        -2.0 * jnp.arange(HEAD_SIZE // 2, dtype=jnp.float32) / HEAD_SIZE
    )
    angles = position.astype(jnp.float32)[:, None] * frequencies[None, :]
    cosine, sine = jnp.cos(angles), jnp.sin(angles)
    cosine = jnp.concatenate([cosine, cosine], axis=1)
    sine = jnp.concatenate([-sine, sine], axis=1)

    gain = norm_gain.reshape(2, half)
    kv_bias = jnp.concatenate(
        [
            lax.dynamic_slice_in_dim(key_bias, plane * HEAD_SIZE, HEAD_SIZE, 0),
            lax.dynamic_slice_in_dim(value_bias, plane * HEAD_SIZE, HEAD_SIZE, 0),
        ]
    ).astype(jnp.float32)[None]
    def slot(number, near, far):
        flags = jnp.stack([tp_index, order[number]])
        return do_slot(flags, source, near, far, kv_families, gain, kv_bias, cosine, sine)

    inside = (plane != 0) & (plane != PLANES - 1)
    phase = lax.optimization_barrier
    near1, swap_in = pair_planes(hidden_in, 0), pair_planes(hidden_in, 1)
    far0 = across(hidden_in)
    near1, swap_in, far0, kv_send, cosine, sine, *query_send = phase(
        (near1, swap_in, far0, kv_send, cosine, sine, *query_send)
    )

    swap_2a, swap_2b = pair_planes(swap_in, 0), pair_planes(near1, 1)
    far1 = across(near1)
    kv_a = exchange(kv_send)
    swap_in, swap_2a, swap_2b, far1, kv_a, *query_send = phase(
        (swap_in, swap_2a, swap_2b, far1, kv_a, *query_send)
    )

    swap_3 = pair_planes(swap_2b, 0)
    near2 = jnp.where(inside, swap_in, swap_2a)
    far2 = across(near2)
    kv_b, kv_c = swap(kv_a, 2), swap(kv_a, 1)
    kv_d = swap(kv_b, 1)
    q0_a = exchange(query_send[0])
    swap_2b, swap_3, near2, far2, kv_b, kv_c, kv_d, q0_a, *query_send = phase(
        (swap_2b, swap_3, near2, far2, kv_b, kv_c, kv_d, q0_a, *query_send)
    )

    kv_families = (kv_a, kv_b, kv_c, kv_d)
    near3 = jnp.where(inside, swap_2b, swap_3)
    far3 = across(near3)
    q0_b, q0_c = swap(q0_a, 2), swap(q0_a, 1)
    q1_a = exchange(query_send[1])
    q2_a = exchange(hold(query_send[2], q1_a))
    early, early_kv = zip(
        slot(0, hidden_in, far0), slot(1, near1, far1), slot(2, near2, far2)
    )
    early_kv = [jnp.concatenate(early_kv, axis=0)]
    early_kv += [swap(early_kv[0], 2), swap(early_kv[0], 1)]
    early_kv.append(swap(early_kv[1], 1))
    q0_b, early = phase((q0_b, early))
    q0_d = swap(q0_b, 1)
    q1_b, q1_c = swap(hold(q1_a, q0_b), 2), swap(q1_a, 1)
    q1_d = swap(q1_b, 1)
    far3, near3, q0_b, q0_c, q2_a, early, early_kv[1], *query_send = phase(
        (far3, near3, q0_b, q0_c, q2_a, early, early_kv[1], *query_send)
    )

    last, late_kv = slot(3, near3, far3)
    slots = [*early, last]
    kv_all = [*early_kv, late_kv] + [swap(late_kv, bits) for bits in (2, 1, 3)]
    q2_b, q2_c = swap(q2_a, 2), swap(q2_a, 1)
    q3_a = exchange(query_send[3])
    places = (order[None, :] * INNER + source[:, None]).reshape(-1)

    per_rows = rows // BLK
    blocks = (
        (each * INNER + inner)[:, None] * per_rows
        + jnp.arange(per_rows, dtype=jnp.int32)[None, :]
    ).reshape(-1)
    block_ids = jnp.arange(nblocks, dtype=jnp.int32)
    same = block_segment[:, None] == block_segment[None, :]
    leading = jnp.min(jnp.where(same, block_ids[None, :], nblocks), axis=1).astype(jnp.int32)
    prompt = blocks < nblocks // 2
    per_tile = TILE // BLK
    full_tiles = jnp.where(prompt, blocks // per_tile, nblocks // 2 // per_tile)
    tail = jnp.where(prompt, blocks // per_tile * per_tile, lookup(leading, blocks))
    facts = jnp.concatenate([blocks, full_tiles, tail]).astype(jnp.int32)

    def queries_of(number, families):
        columns = w_query.shape[1] // PLANES // 2
        bias = lax.dynamic_slice_in_dim(
            q_bias, plane * head_columns + number * columns, columns, 0
        )
        return project(
            order, source, slots, families, bias.astype(jnp.float32)[None], cosine, sine
        )

    def attended_by(queries, distances):
        chunks = plane ^ jnp.asarray(distances, jnp.int32)
        done = attend(facts, places, chunks, queries, kv_all, nblocks * BLK)
        return [
            lax.slice_in_dim(done, k * rows, (k + 1) * rows, axis=0)
            for k in range(len(distances))
        ]

    queries_a = queries_of(0, (q0_a, q0_b, q0_c, q0_d, q1_a, q1_b, q1_c, q1_d))
    q2_b, q3_a, queries_a, kv_all = phase((q2_b, q3_a, queries_a, kv_all))
    q3_b, q3_c, q2_d = swap(q3_a, 2), swap(q3_a, 1), swap(q2_b, 1)
    far, near, beside, own = attended_by(queries_a, (3, 2, 1, 0))
    q3_b, far, near, beside, own = phase((q3_b, far, near, beside, own))
    q3_d = swap(q3_b, 1)
    finished = [swap(far, 3 * INNER), swap(near, 2 * INNER), swap(beside, INNER), own]
    queries_b = queries_of(1, (q2_a, q2_b, q2_c, q2_d, q3_a, q3_b, q3_c, q3_d))
    queries_b, finished = phase((queries_b, finished))
    far, near = attended_by(queries_b, (3, 2))
    queries_b, far, near = phase((queries_b, far, near))
    finished += [swap(far, 3 * INNER), swap(near, 2 * INNER)]
    beside, own = attended_by(queries_b, (1, 0))
    finished += [swap(beside, INNER), own]
    columns_at = [
        (plane ^ m) * head_columns + offset
        for offset in (0, head_columns // 2)
        for m in (3, 2, 1, 0)
    ]
    return collect(jnp.stack(columns_at), finished, w_query.shape[1])


def solution(mesh):
    placed = (
        P("ctx", "tp"),
        P(),
        P("ctx", "tp"),
        P("tp"),
        P("ctx", "tp"),
        P("tp"),
        P("ctx", "tp"),
        P("tp"),
        P(),
        P(),
    )
    planes = mesh.shape["ctx"] == PLANES * INNER and mesh.shape["tp"] == 2
    return jax.shard_map(
        by_planes if planes else local,
        mesh=mesh,
        in_specs=placed,
        out_specs=P("ctx", "tp"),
        check_vma=False,
    )
```

```python
import math

import jax
import jax.numpy as jnp
from jax import lax
from jax.experimental import pallas as pl
from jax.experimental.pallas import tpu as pltpu
from jax.sharding import PartitionSpec as P

HEAD_SIZE = 128
BLK = 128


ROPE_THETA = 1000000.0
EPSILON = 1e-06
NEG_FILL = -1e30


def rms_norm(rows, gain):
    widened = rows.astype(jnp.float32)
    mean_square = jnp.mean(widened * widened, axis=-1, keepdims=True)
    return (widened * lax.rsqrt(mean_square + EPSILON) * gain).astype(jnp.bfloat16)


def apply_rotation(vectors, token_position):
    half = vectors.shape[-1] // 2
    frequencies = ROPE_THETA ** (-2.0 * jnp.arange(half, dtype=jnp.float32) / vectors.shape[-1])
    angles = token_position.astype(jnp.float32)[:, None] * frequencies[None, :]
    cosine = jnp.cos(angles)[:, None, :]
    sine = jnp.sin(angles)[:, None, :]
    former = vectors[..., :half]
    latter = vectors[..., half:]
    return jnp.concatenate(
        [former * cosine - latter * sine, latter * cosine + former * sine], axis=-1
    )


def lookup(table, index):
    width = table.shape[0]
    hits = index[:, None] == jnp.arange(width, dtype=jnp.int32)[None, :]
    return jnp.sum(jnp.where(hits, table[None, :], 0), axis=1)


def token_facts(token_ids, block_segment):
    count = block_segment.shape[0]
    block_ids = jnp.arange(count, dtype=jnp.int32)
    same = block_segment[:, None] == block_segment[None, :]
    leading = jnp.min(jnp.where(same, block_ids[None, :], count), axis=1)
    blocks = token_ids // BLK
    segment = lookup(block_segment, blocks)
    token_position = jnp.where(
        segment == 0, token_ids, count // 2 * BLK + token_ids - lookup(leading, blocks) * BLK
    )
    return (token_position, segment)


def local(
    hidden_in,
    norm_gain,
    w_query,
    q_bias,
    w_key,
    key_bias,
    value_weight,
    value_bias,
    block_segment,
    key_blocks,
):
    rows_dev = hidden_in.shape[0]
    ctx_index = lax.axis_index("ctx")
    nblocks = block_segment.shape[0]
    heads_q = w_query.shape[1] // HEAD_SIZE
    heads_kv = w_key.shape[1] // HEAD_SIZE
    query_group = heads_q // heads_kv
    scale = HEAD_SIZE ** (-0.5)
    block_ids = jnp.arange(nblocks, dtype=jnp.int32)
    whole = lax.all_gather(hidden_in, "tp", axis=1, tiled=True)
    normed = rms_norm(whole, norm_gain)
    own_tokens = ctx_index * rows_dev + jnp.arange(rows_dev, dtype=jnp.int32)
    own_position, own_segment = token_facts(own_tokens, block_segment)
    listed = jnp.any(key_blocks[:, :, None] == block_ids[None, None, :], axis=1).astype(jnp.float32)

    def add_rows(piece):
        return jnp.dot(normed, piece, preferred_element_type=jnp.float32)

    key_total = add_rows(lax.all_gather(w_key, "ctx", axis=0, tiled=True))
    value_total = add_rows(lax.all_gather(value_weight, "ctx", axis=0, tiled=True))
    lifted = (key_total + key_bias.astype(jnp.float32)).reshape(rows_dev, heads_kv, HEAD_SIZE)
    key_matrix = (
        apply_rotation(lifted, own_position)
        .astype(jnp.bfloat16)
        .reshape(rows_dev, heads_kv * HEAD_SIZE)
    )
    value_matrix = (value_total + value_bias.astype(jnp.float32)).astype(jnp.bfloat16)
    key_matrix, value_matrix = (key_matrix, value_matrix)
    total = add_rows(lax.all_gather(w_query, "ctx", axis=0, tiled=True))
    lifted = (total + q_bias.astype(jnp.float32)).reshape(rows_dev, heads_q, HEAD_SIZE)
    queries = apply_rotation(lifted, own_position).astype(jnp.bfloat16)
    query_position, query_segment = token_facts(own_tokens, block_segment)
    query_onehot = ((own_tokens // BLK)[:, None] == block_ids[None, :]).astype(jnp.float32)
    query_listed = jnp.dot(query_onehot, listed, preferred_element_type=jnp.float32)
    arranged = (
        queries.reshape(rows_dev, heads_kv, query_group, HEAD_SIZE)
        .transpose(1, 2, 0, 3)
        .reshape(heads_kv, query_group * rows_dev, HEAD_SIZE)
    )
    initial = (
        jnp.full((heads_kv, query_group * rows_dev), NEG_FILL, jnp.float32),
        jnp.zeros((heads_kv, query_group * rows_dev), jnp.float32),
        jnp.zeros((heads_kv, query_group * rows_dev, HEAD_SIZE), jnp.float32),
    )

    def visit(state, key_tile, value_tile, tile_tokens):
        tile_blocks = tile_tokens // BLK
        tile_onehot = (tile_blocks[:, None] == block_ids[None, :]).astype(jnp.float32)
        in_list = jnp.dot(query_listed, tile_onehot.T, preferred_element_type=jnp.float32) > 0.5
        tile_segment = lookup(block_segment, tile_blocks)
        visible = in_list & (
            (query_segment[:, None] != tile_segment[None, :])
            | (tile_tokens[None, :] <= own_tokens[:, None])
        )

        def update(current):
            peak, denominator, accumulated = current
            scores = (
                jnp.einsum(
                    "gqd,kgd->gqk",
                    arranged,
                    key_tile.reshape(-1, heads_kv, HEAD_SIZE),
                    preferred_element_type=jnp.float32,
                )
                * scale
            )
            mask = jnp.tile(visible, (query_group, 1))[None]
            new_peak = jnp.maximum(peak, jnp.max(jnp.where(mask, scores, NEG_FILL), axis=-1))
            weights = jnp.where(mask, jnp.exp(scores - new_peak[..., None]), 0.0)
            factor = jnp.exp(peak - new_peak)
            denominator = denominator * factor + jnp.sum(weights, axis=-1)
            accumulated = accumulated * factor[..., None] + jnp.einsum(
                "gqk,kgd->gqd",
                weights.astype(jnp.bfloat16),
                value_tile.reshape(-1, heads_kv, HEAD_SIZE),
                preferred_element_type=jnp.float32,
            )
            return (new_peak, denominator, accumulated)

        def keep(current):
            return current

        return lax.cond(jnp.any(visible), update, keep, state)

    key_piece = lax.all_gather(key_matrix, "ctx", axis=0, tiled=True)
    value_piece = lax.all_gather(value_matrix, "ctx", axis=0, tiled=True)
    count = key_piece.shape[0]
    span = math.gcd(count, 512)
    steps = count // span

    def one_step(index, state):
        offset = index * span
        key_tile = lax.dynamic_slice_in_dim(key_piece, offset, span, 0)
        value_tile = lax.dynamic_slice_in_dim(value_piece, offset, span, 0)
        tile_tokens = 0 + offset + jnp.arange(span, dtype=jnp.int32)
        return visit(state, key_tile, value_tile, tile_tokens)

    final_state = lax.fori_loop(0, steps, one_step, initial)
    peak, denominator, accumulated = final_state
    attended = (accumulated / denominator[..., None]).reshape(
        heads_kv, query_group, rows_dev, HEAD_SIZE
    )
    attended = (
        attended.transpose(2, 0, 1, 3).reshape(rows_dev, heads_q * HEAD_SIZE).astype(jnp.bfloat16)
    )
    return attended


PLANES = 4
INNER = 4
TILE = 512
VMEM_BYTES = 60 << 20
COLUMNS = 256


def hold(value, *others):
    return lax.optimization_barrier((value,) + others)[0]


def fetch_weights(source, families, weight_buf, sems):
    depth = families[0].shape[0] // PLANES
    copies = [[] for _ in range(PLANES)]
    for f, family in enumerate(families):
        columns = family.shape[1]
        first = f // INNER * columns
        for z in range(PLANES):
            start = pl.multiple_of((z * INNER + source[f % INNER]) * depth, depth)
            copies[z].append(
                pltpu.make_async_copy(
                    family.at[pl.ds(z * depth, depth), :],
                    weight_buf.at[pl.ds(start, depth), pl.ds(first, columns)],
                    sems.at[f * PLANES + z],
                )
            )
    return copies


def rotate(part, turn_cos, turn_sin):
    return part * turn_cos + pltpu.roll(part, HEAD_SIZE // 2, 1) * turn_sin


def slot_kernel(
    flags, source, near, far, w0, w1, w2, w3, gain, bias, cosine, sine, out, kv, weight_buf, sems
):
    copies = sum(fetch_weights(source, (w0, w1, w2, w3), weight_buf, sems), [])
    for copy in copies:
        copy.start()
    rows, half = near.shape
    step = 32
    mine = flags[0]

    def chunk(i, carry):
        at = pl.multiple_of(i * step, step)
        left = near[pl.ds(at, step), :].astype(jnp.float32)
        right = far[pl.ds(at, step), :].astype(jnp.float32)
        total = jnp.sum(left * left, axis=-1, keepdims=True) + jnp.sum(
            right * right, axis=-1, keepdims=True
        )
        factor = lax.rsqrt(total * (0.5 / half) + EPSILON)
        out[mine, pl.ds(at, step), :] = (left * factor * gain[pl.ds(mine, 1), :]).astype(
            jnp.bfloat16
        )
        out[1 - mine, pl.ds(at, step), :] = (right * factor * gain[pl.ds(1 - mine, 1), :]).astype(
            jnp.bfloat16
        )
        return carry

    lax.fori_loop(0, rows // step, chunk, 0)
    for copy in copies:
        copy.wait()
    total = jnp.dot(out[0], weight_buf[:half, :], preferred_element_type=jnp.float32) + jnp.dot(
        out[1], weight_buf[half:, :], preferred_element_type=jnp.float32
    )
    total = total + bias[...]
    start = pl.multiple_of(flags[1] * rows, rows)
    key = rotate(total[:, :HEAD_SIZE], cosine[pl.ds(start, rows), :], sine[pl.ds(start, rows), :])
    kv[:, :HEAD_SIZE] = key.astype(jnp.bfloat16)
    kv[:, HEAD_SIZE:] = total[:, HEAD_SIZE:].astype(jnp.bfloat16)


def do_slot(flags, source, near, far, families, gain, bias, cosine, sine):
    rows, half = near.shape
    columns = families[0].shape[1]
    in_vmem = pl.BlockSpec(memory_space=pltpu.VMEM)
    anywhere = pl.BlockSpec(memory_space=pl.ANY)
    scalars = pl.BlockSpec(memory_space=pltpu.SMEM)
    return pl.pallas_call(
        slot_kernel,
        out_shape=(
            jax.ShapeDtypeStruct((2, rows, half), jnp.bfloat16),
            jax.ShapeDtypeStruct((rows, columns), jnp.bfloat16),
        ),
        in_specs=[scalars, scalars, in_vmem, in_vmem] + [anywhere] * INNER + [in_vmem] * 4,
        out_specs=(in_vmem, in_vmem),
        scratch_shapes=[
            pltpu.VMEM((2 * half, columns), jnp.bfloat16),
            pltpu.SemaphoreType.DMA((4 * PLANES,)),
        ],
        compiler_params=pltpu.CompilerParams(vmem_limit_bytes=VMEM_BYTES),
        cost_estimate=pl.CostEstimate(
            flops=4 * rows * half * columns,
            transcendentals=0,
            bytes_accessed=8 * rows * half + 4 * half * columns,
        ),
        name="slot",
    )(flags, source, near, far, *families, gain, bias, cosine, sine)


def project_kernel(order, source, *refs):
    slots, families = refs[:PLANES], refs[PLANES:-9]
    bias, cosine, sine, out, rows_buf, weight_buf, total, row_sems, weight_sems = refs[-9:]
    rows, half = slots[0].shape[1:]
    columns = out.shape[1]
    depth = half * 2 // PLANES
    chunks = fetch_weights(source, families, weight_buf, weight_sems)
    for z, chunk in enumerate(chunks):
        part = (z * depth) // half
        within = z * depth - part * half
        for s in range(PLANES):
            chunk.append(
                pltpu.make_async_copy(
                    slots[s].at[part, :, pl.ds(within, depth)],
                    rows_buf.at[z, pl.ds(s * rows, rows), :],
                    row_sems.at[z * PLANES + s],
                )
            )
        for copy in chunk:
            copy.start()
    for z, chunk in enumerate(chunks):
        for copy in chunk:
            copy.wait()
        product = jnp.dot(
            rows_buf[z],
            weight_buf[z * depth : (z + 1) * depth, :],
            preferred_element_type=jnp.float32,
        )
        if z == 0:
            total[...] = product
        elif z < PLANES - 1:
            total[...] += product
        else:
            total[...] = total[...] + product + bias[...]
    for s in range(PLANES):
        start = pl.multiple_of(order[s] * rows, rows)
        turn_cos = cosine[pl.ds(start, rows), :]
        turn_sin = sine[pl.ds(start, rows), :]
        for h in range(columns // HEAD_SIZE):
            part = total[s * rows : (s + 1) * rows, h * HEAD_SIZE : (h + 1) * HEAD_SIZE]
            out[pl.ds(start, rows), h * HEAD_SIZE : (h + 1) * HEAD_SIZE] = rotate(
                part, turn_cos, turn_sin
            ).astype(jnp.bfloat16)


def project(order, source, slots, families, bias, cosine, sine):
    rows, half = slots[0].shape[1:]
    columns = families[0].shape[1] * (len(families) // INNER)
    in_vmem = pl.BlockSpec(memory_space=pltpu.VMEM)
    anywhere = pl.BlockSpec(memory_space=pl.ANY)
    scalars = pl.BlockSpec(memory_space=pltpu.SMEM)
    return pl.pallas_call(
        project_kernel,
        out_shape=jax.ShapeDtypeStruct((PLANES * rows, columns), jnp.bfloat16),
        in_specs=[scalars, scalars] + [anywhere] * (PLANES + len(families)) + [in_vmem] * 3,
        out_specs=in_vmem,
        scratch_shapes=[
            pltpu.VMEM((PLANES, PLANES * rows, 2 * half // PLANES), jnp.bfloat16),
            pltpu.VMEM((2 * half, columns), jnp.bfloat16),
            pltpu.VMEM((PLANES * rows, columns), jnp.float32),
            pltpu.SemaphoreType.DMA((PLANES * PLANES,)),
            pltpu.SemaphoreType.DMA((len(families) * PLANES,)),
        ],
        compiler_params=pltpu.CompilerParams(vmem_limit_bytes=VMEM_BYTES),
        cost_estimate=pl.CostEstimate(
            flops=2 * PLANES * rows * 2 * half * columns,
            transcendentals=0,
            bytes_accessed=2 * (PLANES * rows * 2 * half + 2 * half * columns),
        ),
        name="project",
    )(order, source, *slots, *families, bias, cosine, sine)


def attend_kernel(total_rows, facts, places, chunks, queries, *refs):
    pieces = refs[: 2 * INNER]
    out, key_buf, value_buf, sems = refs[2 * INNER :]
    at = pl.program_id(0)
    rows = pieces[-1].shape[0]
    heads = queries.shape[1] // HEAD_SIZE

    @pl.when(at == 0)
    def load():
        copies = []
        for p in range(INNER):
            for m in range(PLANES):
                start = pl.multiple_of(places[p * PLANES + m] * rows, rows)
                late = m == PLANES - 1
                for part, buf in ((0, key_buf), (1, value_buf)):
                    copies.append(
                        pltpu.make_async_copy(
                            pieces[p + INNER if late else p].at[
                                pl.ds(0 if late else m * rows, rows),
                                pl.ds(part * HEAD_SIZE, HEAD_SIZE),
                            ],
                            buf.at[pl.ds(start, rows), pl.ds(0, HEAD_SIZE)],
                            sems.at[(p * PLANES + m) * 2 + part],
                        )
                    )
        for copy in copies:
            copy.start()
        extra = key_buf.shape[0] - total_rows
        key_buf[total_rows:, :] = jnp.zeros((extra, HEAD_SIZE), jnp.bfloat16)
        value_buf[total_rows:, :HEAD_SIZE] = jnp.zeros((extra, HEAD_SIZE), jnp.bfloat16)
        value_buf[:, HEAD_SIZE:] = jnp.ones((key_buf.shape[0], HEAD_SIZE), jnp.bfloat16)
        for copy in copies:
            copy.wait()

    per_step = queries.shape[0] // BLK
    count = total_rows // INNER // BLK
    first_block = chunks[at] * per_step
    full_tiles = facts[count + first_block]
    exponent = HEAD_SIZE ** (-0.5) * math.log2(math.e)
    chains = [(p, j) for p in range(per_step) for j in range(heads // 2)]

    def part(p, h):
        return (slice(p * BLK, (p + 1) * BLK), slice(h * HEAD_SIZE, (h + 1) * HEAD_SIZE))

    stacked = [
        jnp.concatenate([queries[part(p, 2 * j)], queries[part(p, 2 * j + 1)]], axis=0)
        for p, j in chains
    ]
    lines = 2 * BLK

    def update(state, number, keys, values, visible):
        peak, held = state
        scores = lax.dot_general(
            stacked[number], keys, (((1,), (1,)), ((), ())), preferred_element_type=jnp.float32
        )
        if visible is not None:
            scores = jnp.where(visible, scores, NEG_FILL)
        new_peak = jnp.maximum(peak, jnp.max(scores, axis=-1, keepdims=True))
        weights = jnp.exp2((scores - new_peak) * exponent)
        factor = jnp.exp2((peak - new_peak) * exponent)
        held = held * factor + jnp.dot(
            weights.astype(jnp.bfloat16), values, preferred_element_type=jnp.float32
        )
        return new_peak, held

    def tiles(start, size, state):
        keys, values = key_buf[pl.ds(start, size), :], value_buf[pl.ds(start, size), :]
        return tuple(update(one, n, keys, values, None) for n, one in enumerate(state))

    def double_tile(t, state):
        return tiles(pl.multiple_of(t * 2 * TILE, 2 * TILE), 2 * TILE, state)

    def odd_tile(t, state):
        return tiles(pl.multiple_of((full_tiles - 1) * TILE, TILE), TILE, state)

    state = tuple(
        (
            jnp.full((lines, 1), NEG_FILL, jnp.float32),
            jnp.zeros((lines, 2 * HEAD_SIZE), jnp.float32),
        )
        for _ in chains
    )
    state = lax.fori_loop(0, full_tiles // 2, double_tile, state)
    state = lax.fori_loop(0, full_tiles % 2, odd_tile, state)
    line = lax.broadcasted_iota(jnp.int32, (lines, TILE), 0) % BLK
    column = lax.broadcasted_iota(jnp.int32, (lines, TILE), 1)
    for number, (p, j) in enumerate(chains):
        block = facts[first_block + p]
        tail = pl.multiple_of(facts[2 * count + first_block + p] * BLK, BLK)
        keys, values = key_buf[pl.ds(tail, TILE), :], value_buf[pl.ds(tail, TILE), :]
        visible = column - line <= block * BLK - tail
        held = update(state[number], number, keys, values, visible)[1]
        done = (held[:, :HEAD_SIZE] / held[:, HEAD_SIZE:]).astype(jnp.bfloat16)
        out[part(p, 2 * j)] = done[:BLK]
        out[part(p, 2 * j + 1)] = done[BLK:]


def attend(facts, places, chunks, queries, pieces, total_rows):
    columns = queries.shape[1]
    step = queries.shape[0] // PLANES
    count = chunks.shape[0] * step

    def kernel(*refs):
        attend_kernel(total_rows, *refs)

    return pl.pallas_call(
        kernel,
        out_shape=jax.ShapeDtypeStruct((count, columns), jnp.bfloat16),
        grid_spec=pltpu.PrefetchScalarGridSpec(
            num_scalar_prefetch=3,
            grid=(chunks.shape[0],),
            in_specs=[pl.BlockSpec((step, columns), lambda i, a, b, c: (c[i], 0))]
            + [pl.BlockSpec(memory_space=pl.ANY)] * (2 * INNER),
            out_specs=pl.BlockSpec((step, columns), lambda i, a, b, c: (i, 0)),
            scratch_shapes=[
                pltpu.VMEM((total_rows + TILE - BLK, HEAD_SIZE), jnp.bfloat16),
                pltpu.VMEM((total_rows + TILE - BLK, 2 * HEAD_SIZE), jnp.bfloat16),
                pltpu.SemaphoreType.DMA((INNER * PLANES * 2,)),
            ],
        ),
        compiler_params=pltpu.CompilerParams(vmem_limit_bytes=VMEM_BYTES),
        cost_estimate=pl.CostEstimate(
            flops=4 * count * columns * (total_rows // 2),
            transcendentals=count * (columns // HEAD_SIZE) * (total_rows // 2),
            bytes_accessed=4 * count * columns + 2 * total_rows * 2 * HEAD_SIZE,
        ),
        name="attend",
    )(facts, places, chunks, queries, *pieces)


def collect_kernel(places, *refs):
    pieces, out = refs[:-1], refs[-1]
    for k, piece in enumerate(pieces):
        start = pl.multiple_of(places[k], HEAD_SIZE)
        out[:, pl.ds(start, piece.shape[1])] = piece[...]


def collect(places, pieces, columns):
    in_vmem = pl.BlockSpec(memory_space=pltpu.VMEM)
    return pl.pallas_call(
        collect_kernel,
        out_shape=jax.ShapeDtypeStruct((pieces[0].shape[0], columns), jnp.bfloat16),
        in_specs=[pl.BlockSpec(memory_space=pltpu.SMEM)] + [in_vmem] * len(pieces),
        out_specs=in_vmem,
        name="collect",
    )(places, *pieces)


def by_planes(
    hidden_in,
    norm_gain,
    w_query,
    q_bias,
    w_key,
    key_bias,
    value_weight,
    value_bias,
    block_segment,
    key_blocks,
):
    devices = PLANES * INNER
    ctx_index = lax.axis_index("ctx").astype(jnp.int32)
    tp_index = lax.axis_index("tp").astype(jnp.int32)
    plane = ctx_index // INNER
    inner = ctx_index % INNER
    rows, half = hidden_in.shape
    nblocks = block_segment.shape[0]
    head_columns = w_query.shape[1] // PLANES

    def swap(array, bits):
        return lax.ppermute(array, "ctx", [(i, i ^ bits) for i in range(devices)])

    def pair_planes(array, low):
        def partner(i):
            z = i // INNER
            to = low + ((z - low) ^ 1)
            return i + (to - z) * INNER if low <= z and 0 <= to < PLANES else i

        return lax.ppermute(
            array, "ctx", [(i, partner(i)) for i in range(devices) if partner(i) != i]
        )

    def across(array):
        return lax.ppermute(array, "tp", [(0, 1), (1, 0)])

    def exchange(array):
        return lax.all_to_all(
            array,
            "ctx",
            0,
            0,
            axis_index_groups=[
                [z * INNER + r for z in range(PLANES)] for r in range(INNER)
            ],
            tiled=True,
        )

    def stacked_columns(array, stride, offset, columns):
        return [
            lax.slice_in_dim(array, z * stride + offset, z * stride + offset + columns, axis=1)
            for z in range(PLANES)
        ]

    kv_send = jnp.concatenate(
        [
            jnp.concatenate(pair, axis=1)
            for pair in zip(
                stacked_columns(w_key, HEAD_SIZE, 0, HEAD_SIZE),
                stacked_columns(value_weight, HEAD_SIZE, 0, HEAD_SIZE),
            )
        ],
        axis=0,
    )
    query_send = [
        jnp.concatenate(stacked_columns(w_query, head_columns, offset, COLUMNS), axis=0)
        for offset in range(0, head_columns, COLUMNS)
    ]
    table = jnp.asarray([[0, 1, 2, 3], [1, 0, 2, 3], [2, 3, 1, 0], [3, 2, 1, 0]], jnp.int32)
    order = lax.dynamic_index_in_dim(table, plane, 0, keepdims=False)
    bits = jnp.asarray([0, 2, 1, 3], jnp.int32)
    source = inner ^ bits

    each = jnp.arange(PLANES, dtype=jnp.int32)
    tokens = (
        (each * (INNER * rows) + inner * rows)[:, None]
        + jnp.arange(rows, dtype=jnp.int32)[None, :]
    ).reshape(-1)
    position, _ = token_facts(tokens, block_segment)
    frequencies = ROPE_THETA ** (
        -2.0 * jnp.arange(HEAD_SIZE // 2, dtype=jnp.float32) / HEAD_SIZE
    )
    angles = position.astype(jnp.float32)[:, None] * frequencies[None, :]
    cosine, sine = jnp.cos(angles), jnp.sin(angles)
    cosine = jnp.concatenate([cosine, cosine], axis=1)
    sine = jnp.concatenate([-sine, sine], axis=1)

    gain = norm_gain.reshape(2, half)
    kv_bias = jnp.concatenate(
        [
            lax.dynamic_slice_in_dim(key_bias, plane * HEAD_SIZE, HEAD_SIZE, 0),
            lax.dynamic_slice_in_dim(value_bias, plane * HEAD_SIZE, HEAD_SIZE, 0),
        ]
    ).astype(jnp.float32)[None]
    def slot(number, near, far):
        flags = jnp.stack([tp_index, order[number]])
        return do_slot(flags, source, near, far, kv_families, gain, kv_bias, cosine, sine)

    inside = (plane != 0) & (plane != PLANES - 1)
    phase = lax.optimization_barrier
    near1, swap_in = pair_planes(hidden_in, 0), pair_planes(hidden_in, 1)
    far0 = across(hidden_in)
    near1, swap_in, far0, kv_send, cosine, sine, *query_send = phase(
        (near1, swap_in, far0, kv_send, cosine, sine, *query_send)
    )

    swap_2a, swap_2b = pair_planes(swap_in, 0), pair_planes(near1, 1)
    far1 = across(near1)
    kv_a = exchange(kv_send)
    swap_in, swap_2a, swap_2b, far1, kv_a, *query_send = phase(
        (swap_in, swap_2a, swap_2b, far1, kv_a, *query_send)
    )

    swap_3 = pair_planes(swap_2b, 0)
    near2 = jnp.where(inside, swap_in, swap_2a)
    far2 = across(near2)
    kv_b, kv_c = swap(kv_a, 2), swap(kv_a, 1)
    kv_d = swap(kv_b, 1)
    q0_a = exchange(query_send[0])
    swap_2b, swap_3, near2, far2, kv_b, kv_c, kv_d, q0_a, *query_send = phase(
        (swap_2b, swap_3, near2, far2, kv_b, kv_c, kv_d, q0_a, *query_send)
    )

    kv_families = (kv_a, kv_b, kv_c, kv_d)
    near3 = jnp.where(inside, swap_2b, swap_3)
    far3 = across(near3)
    q0_b, q0_c = swap(q0_a, 2), swap(q0_a, 1)
    q1_a = exchange(query_send[1])
    q2_a = exchange(hold(query_send[2], q1_a))
    early_0 = slot(0, hidden_in, far0)
    near1, far1, q1_a, q0_b = phase((near1, far1, q1_a, q0_b))
    early, early_kv = zip(early_0, slot(1, near1, far1), slot(2, near2, far2))
    early_kv = [jnp.concatenate(early_kv, axis=0)]
    early_kv += [swap(early_kv[0], 2), swap(early_kv[0], 1)]
    early_kv.append(swap(early_kv[1], 1))
    q0_b, early = phase((q0_b, early))
    q0_d = swap(q0_b, 1)
    q1_b, q1_c = swap(q1_a, 2), swap(q1_a, 1)
    q1_d = swap(q1_b, 1)
    far3, near3, q0_b, q0_c, q2_a, early, *query_send = phase(
        (far3, near3, q0_b, q0_c, q2_a, early, *query_send)
    )

    last, late_kv = slot(3, near3, far3)
    slots = [*early, last]
    kv_all = [*early_kv, late_kv] + [swap(late_kv, bits) for bits in (2, 1, 3)]
    q2_b, q2_c = swap(q2_a, 2), swap(q2_a, 1)
    q3_a = exchange(query_send[3])
    places = (order[None, :] * INNER + source[:, None]).reshape(-1)

    per_rows = rows // BLK
    blocks = (
        (each * INNER + inner)[:, None] * per_rows
        + jnp.arange(per_rows, dtype=jnp.int32)[None, :]
    ).reshape(-1)
    block_ids = jnp.arange(nblocks, dtype=jnp.int32)
    same = block_segment[:, None] == block_segment[None, :]
    leading = jnp.min(jnp.where(same, block_ids[None, :], nblocks), axis=1).astype(jnp.int32)
    prompt = blocks < nblocks // 2
    per_tile = TILE // BLK
    full_tiles = jnp.where(prompt, blocks // per_tile, nblocks // 2 // per_tile)
    tail = jnp.where(prompt, blocks // per_tile * per_tile, lookup(leading, blocks))
    facts = jnp.concatenate([blocks, full_tiles, tail]).astype(jnp.int32)

    def queries_of(number, families):
        columns = w_query.shape[1] // PLANES // 2
        bias = lax.dynamic_slice_in_dim(
            q_bias, plane * head_columns + number * columns, columns, 0
        )
        return project(
            order, source, slots, families, bias.astype(jnp.float32)[None], cosine, sine
        )

    def attended_by(queries, distances):
        chunks = plane ^ jnp.asarray(distances, jnp.int32)
        done = attend(facts, places, chunks, queries, kv_all, nblocks * BLK)
        return [
            lax.slice_in_dim(done, k * rows, (k + 1) * rows, axis=0)
            for k in range(len(distances))
        ]

    queries_a = queries_of(0, (q0_a, q0_b, q0_c, q0_d, q1_a, q1_b, q1_c, q1_d))
    q2_b, q3_a, queries_a, kv_all = phase((q2_b, q3_a, queries_a, kv_all))
    q3_b, q3_c, q2_d = swap(q3_a, 2), swap(q3_a, 1), swap(q2_b, 1)
    far, near, beside, own = attended_by(queries_a, (3, 2, 1, 0))
    q3_b, far, near, beside, own = phase((q3_b, far, near, beside, own))
    q3_d = swap(q3_b, 1)
    finished = [swap(far, 3 * INNER), swap(near, 2 * INNER), swap(beside, INNER), own]
    queries_b = queries_of(1, (q2_a, q2_b, q2_c, q2_d, q3_a, q3_b, q3_c, q3_d))
    queries_b, finished = phase((queries_b, finished))
    far, near = attended_by(queries_b, (3, 2))
    queries_b, far, near = phase((queries_b, far, near))
    finished += [swap(far, 3 * INNER), swap(near, 2 * INNER)]
    beside, own = attended_by(queries_b, (1, 0))
    beside, finished[4] = phase((beside, finished[4]))
    finished += [swap(beside, INNER), own]
    columns_at = [
        (plane ^ m) * head_columns + offset
        for offset in (0, head_columns // 2)
        for m in (3, 2, 1, 0)
    ]
    return collect(jnp.stack(columns_at), finished, w_query.shape[1])


def solution(mesh):
    placed = (
        P("ctx", "tp"),
        P(),
        P("ctx", "tp"),
        P("tp"),
        P("ctx", "tp"),
        P("tp"),
        P("ctx", "tp"),
        P("tp"),
        P(),
        P(),
    )
    planes = mesh.shape["ctx"] == PLANES * INNER and mesh.shape["tp"] == 2
    return jax.shard_map(
        by_planes if planes else local,
        mesh=mesh,
        in_specs=placed,
        out_specs=P("ctx", "tp"),
        check_vma=False,
    )
```

```python
import math

import jax
import jax.numpy as jnp
from jax import lax
from jax.experimental import pallas as pl
from jax.experimental.pallas import tpu as pltpu
from jax.sharding import PartitionSpec as P

HEAD_SIZE = 128
BLK = 128


ROPE_THETA = 1000000.0
EPSILON = 1e-06
NEG_FILL = -1e30


def rms_norm(rows, gain):
    widened = rows.astype(jnp.float32)
    mean_square = jnp.mean(widened * widened, axis=-1, keepdims=True)
    return (widened * lax.rsqrt(mean_square + EPSILON) * gain).astype(jnp.bfloat16)


def apply_rotation(vectors, token_position):
    half = vectors.shape[-1] // 2
    frequencies = ROPE_THETA ** (-2.0 * jnp.arange(half, dtype=jnp.float32) / vectors.shape[-1])
    angles = token_position.astype(jnp.float32)[:, None] * frequencies[None, :]
    cosine = jnp.cos(angles)[:, None, :]
    sine = jnp.sin(angles)[:, None, :]
    former = vectors[..., :half]
    latter = vectors[..., half:]
    return jnp.concatenate(
        [former * cosine - latter * sine, latter * cosine + former * sine], axis=-1
    )


def lookup(table, index):
    width = table.shape[0]
    hits = index[:, None] == jnp.arange(width, dtype=jnp.int32)[None, :]
    return jnp.sum(jnp.where(hits, table[None, :], 0), axis=1)


def token_facts(token_ids, block_segment):
    count = block_segment.shape[0]
    block_ids = jnp.arange(count, dtype=jnp.int32)
    same = block_segment[:, None] == block_segment[None, :]
    leading = jnp.min(jnp.where(same, block_ids[None, :], count), axis=1)
    blocks = token_ids // BLK
    segment = lookup(block_segment, blocks)
    token_position = jnp.where(
        segment == 0, token_ids, count // 2 * BLK + token_ids - lookup(leading, blocks) * BLK
    )
    return (token_position, segment)


def local(
    hidden_in,
    norm_gain,
    w_query,
    q_bias,
    w_key,
    key_bias,
    value_weight,
    value_bias,
    block_segment,
    key_blocks,
):
    rows_dev = hidden_in.shape[0]
    ctx_index = lax.axis_index("ctx")
    nblocks = block_segment.shape[0]
    heads_q = w_query.shape[1] // HEAD_SIZE
    heads_kv = w_key.shape[1] // HEAD_SIZE
    query_group = heads_q // heads_kv
    scale = HEAD_SIZE ** (-0.5)
    block_ids = jnp.arange(nblocks, dtype=jnp.int32)
    whole = lax.all_gather(hidden_in, "tp", axis=1, tiled=True)
    normed = rms_norm(whole, norm_gain)
    own_tokens = ctx_index * rows_dev + jnp.arange(rows_dev, dtype=jnp.int32)
    own_position, own_segment = token_facts(own_tokens, block_segment)
    listed = jnp.any(key_blocks[:, :, None] == block_ids[None, None, :], axis=1).astype(jnp.float32)

    def add_rows(piece):
        return jnp.dot(normed, piece, preferred_element_type=jnp.float32)

    key_total = add_rows(lax.all_gather(w_key, "ctx", axis=0, tiled=True))
    value_total = add_rows(lax.all_gather(value_weight, "ctx", axis=0, tiled=True))
    lifted = (key_total + key_bias.astype(jnp.float32)).reshape(rows_dev, heads_kv, HEAD_SIZE)
    key_matrix = (
        apply_rotation(lifted, own_position)
        .astype(jnp.bfloat16)
        .reshape(rows_dev, heads_kv * HEAD_SIZE)
    )
    value_matrix = (value_total + value_bias.astype(jnp.float32)).astype(jnp.bfloat16)
    key_matrix, value_matrix = (key_matrix, value_matrix)
    total = add_rows(lax.all_gather(w_query, "ctx", axis=0, tiled=True))
    lifted = (total + q_bias.astype(jnp.float32)).reshape(rows_dev, heads_q, HEAD_SIZE)
    queries = apply_rotation(lifted, own_position).astype(jnp.bfloat16)
    query_position, query_segment = token_facts(own_tokens, block_segment)
    query_onehot = ((own_tokens // BLK)[:, None] == block_ids[None, :]).astype(jnp.float32)
    query_listed = jnp.dot(query_onehot, listed, preferred_element_type=jnp.float32)
    arranged = (
        queries.reshape(rows_dev, heads_kv, query_group, HEAD_SIZE)
        .transpose(1, 2, 0, 3)
        .reshape(heads_kv, query_group * rows_dev, HEAD_SIZE)
    )
    initial = (
        jnp.full((heads_kv, query_group * rows_dev), NEG_FILL, jnp.float32),
        jnp.zeros((heads_kv, query_group * rows_dev), jnp.float32),
        jnp.zeros((heads_kv, query_group * rows_dev, HEAD_SIZE), jnp.float32),
    )

    def visit(state, key_tile, value_tile, tile_tokens):
        tile_blocks = tile_tokens // BLK
        tile_onehot = (tile_blocks[:, None] == block_ids[None, :]).astype(jnp.float32)
        in_list = jnp.dot(query_listed, tile_onehot.T, preferred_element_type=jnp.float32) > 0.5
        tile_segment = lookup(block_segment, tile_blocks)
        visible = in_list & (
            (query_segment[:, None] != tile_segment[None, :])
            | (tile_tokens[None, :] <= own_tokens[:, None])
        )

        def update(current):
            peak, denominator, accumulated = current
            scores = (
                jnp.einsum(
                    "gqd,kgd->gqk",
                    arranged,
                    key_tile.reshape(-1, heads_kv, HEAD_SIZE),
                    preferred_element_type=jnp.float32,
                )
                * scale
            )
            mask = jnp.tile(visible, (query_group, 1))[None]
            new_peak = jnp.maximum(peak, jnp.max(jnp.where(mask, scores, NEG_FILL), axis=-1))
            weights = jnp.where(mask, jnp.exp(scores - new_peak[..., None]), 0.0)
            factor = jnp.exp(peak - new_peak)
            denominator = denominator * factor + jnp.sum(weights, axis=-1)
            accumulated = accumulated * factor[..., None] + jnp.einsum(
                "gqk,kgd->gqd",
                weights.astype(jnp.bfloat16),
                value_tile.reshape(-1, heads_kv, HEAD_SIZE),
                preferred_element_type=jnp.float32,
            )
            return (new_peak, denominator, accumulated)

        def keep(current):
            return current

        return lax.cond(jnp.any(visible), update, keep, state)

    key_piece = lax.all_gather(key_matrix, "ctx", axis=0, tiled=True)
    value_piece = lax.all_gather(value_matrix, "ctx", axis=0, tiled=True)
    count = key_piece.shape[0]
    span = math.gcd(count, 512)
    steps = count // span

    def one_step(index, state):
        offset = index * span
        key_tile = lax.dynamic_slice_in_dim(key_piece, offset, span, 0)
        value_tile = lax.dynamic_slice_in_dim(value_piece, offset, span, 0)
        tile_tokens = 0 + offset + jnp.arange(span, dtype=jnp.int32)
        return visit(state, key_tile, value_tile, tile_tokens)

    final_state = lax.fori_loop(0, steps, one_step, initial)
    peak, denominator, accumulated = final_state
    attended = (accumulated / denominator[..., None]).reshape(
        heads_kv, query_group, rows_dev, HEAD_SIZE
    )
    attended = (
        attended.transpose(2, 0, 1, 3).reshape(rows_dev, heads_q * HEAD_SIZE).astype(jnp.bfloat16)
    )
    return attended


PLANES = 4
INNER = 4
TILE = 512
VMEM_BYTES = 60 << 20
COLUMNS = 256


def hold(value, *others):
    return lax.optimization_barrier((value,) + others)[0]


def fetch_weights(source, families, weight_buf, sems):
    depth = families[0].shape[0] // PLANES
    copies = [[] for _ in range(PLANES)]
    for f, family in enumerate(families):
        columns = family.shape[1]
        first = f // INNER * columns
        for z in range(PLANES):
            start = pl.multiple_of((z * INNER + source[f % INNER]) * depth, depth)
            copies[z].append(
                pltpu.make_async_copy(
                    family.at[pl.ds(z * depth, depth), :],
                    weight_buf.at[pl.ds(start, depth), pl.ds(first, columns)],
                    sems.at[f * PLANES + z],
                )
            )
    return copies


def rotate(part, turn_cos, turn_sin):
    return part * turn_cos + pltpu.roll(part, HEAD_SIZE // 2, 1) * turn_sin


def slot_kernel(
    flags, source, near, far, w0, w1, w2, w3, gain, bias, cosine, sine, out, kv, weight_buf, sems
):
    copies = sum(fetch_weights(source, (w0, w1, w2, w3), weight_buf, sems), [])
    for copy in copies:
        copy.start()
    rows, half = near.shape
    step = 32
    mine = flags[0]

    def chunk(i, carry):
        at = pl.multiple_of(i * step, step)
        left = near[pl.ds(at, step), :].astype(jnp.float32)
        right = far[pl.ds(at, step), :].astype(jnp.float32)
        total = jnp.sum(left * left, axis=-1, keepdims=True) + jnp.sum(
            right * right, axis=-1, keepdims=True
        )
        factor = lax.rsqrt(total * (0.5 / half) + EPSILON)
        out[mine, pl.ds(at, step), :] = (left * factor * gain[pl.ds(mine, 1), :]).astype(
            jnp.bfloat16
        )
        out[1 - mine, pl.ds(at, step), :] = (right * factor * gain[pl.ds(1 - mine, 1), :]).astype(
            jnp.bfloat16
        )
        return carry

    lax.fori_loop(0, rows // step, chunk, 0)
    for copy in copies:
        copy.wait()
    total = jnp.dot(out[0], weight_buf[:half, :], preferred_element_type=jnp.float32) + jnp.dot(
        out[1], weight_buf[half:, :], preferred_element_type=jnp.float32
    )
    total = total + bias[...]
    start = pl.multiple_of(flags[1] * rows, rows)
    key = rotate(total[:, :HEAD_SIZE], cosine[pl.ds(start, rows), :], sine[pl.ds(start, rows), :])
    kv[:, :HEAD_SIZE] = key.astype(jnp.bfloat16)
    kv[:, HEAD_SIZE:] = total[:, HEAD_SIZE:].astype(jnp.bfloat16)


def do_slot(flags, source, near, far, families, gain, bias, cosine, sine):
    rows, half = near.shape
    columns = families[0].shape[1]
    in_vmem = pl.BlockSpec(memory_space=pltpu.VMEM)
    anywhere = pl.BlockSpec(memory_space=pl.ANY)
    scalars = pl.BlockSpec(memory_space=pltpu.SMEM)
    return pl.pallas_call(
        slot_kernel,
        out_shape=(
            jax.ShapeDtypeStruct((2, rows, half), jnp.bfloat16),
            jax.ShapeDtypeStruct((rows, columns), jnp.bfloat16),
        ),
        in_specs=[scalars, scalars, in_vmem, in_vmem] + [anywhere] * INNER + [in_vmem] * 4,
        out_specs=(in_vmem, in_vmem),
        scratch_shapes=[
            pltpu.VMEM((2 * half, columns), jnp.bfloat16),
            pltpu.SemaphoreType.DMA((4 * PLANES,)),
        ],
        compiler_params=pltpu.CompilerParams(vmem_limit_bytes=VMEM_BYTES),
        cost_estimate=pl.CostEstimate(
            flops=4 * rows * half * columns,
            transcendentals=0,
            bytes_accessed=8 * rows * half + 4 * half * columns,
        ),
        name="slot",
    )(flags, source, near, far, *families, gain, bias, cosine, sine)


def project_kernel(order, source, *refs):
    slots, families = refs[:PLANES], refs[PLANES:-9]
    bias, cosine, sine, out, rows_buf, weight_buf, total, row_sems, weight_sems = refs[-9:]
    rows, half = slots[0].shape[1:]
    columns = out.shape[1]
    depth = half * 2 // PLANES
    chunks = fetch_weights(source, families, weight_buf, weight_sems)
    for z, chunk in enumerate(chunks):
        part = (z * depth) // half
        within = z * depth - part * half
        for s in range(PLANES):
            chunk.append(
                pltpu.make_async_copy(
                    slots[s].at[part, :, pl.ds(within, depth)],
                    rows_buf.at[z, pl.ds(s * rows, rows), :],
                    row_sems.at[z * PLANES + s],
                )
            )
        for copy in chunk:
            copy.start()
    for z, chunk in enumerate(chunks):
        for copy in chunk:
            copy.wait()
        product = jnp.dot(
            rows_buf[z],
            weight_buf[z * depth : (z + 1) * depth, :],
            preferred_element_type=jnp.float32,
        )
        if z == 0:
            total[...] = product
        elif z < PLANES - 1:
            total[...] += product
        else:
            total[...] = total[...] + product + bias[...]
    for s in range(PLANES):
        start = pl.multiple_of(order[s] * rows, rows)
        turn_cos = cosine[pl.ds(start, rows), :]
        turn_sin = sine[pl.ds(start, rows), :]
        for h in range(columns // HEAD_SIZE):
            part = total[s * rows : (s + 1) * rows, h * HEAD_SIZE : (h + 1) * HEAD_SIZE]
            out[pl.ds(start, rows), h * HEAD_SIZE : (h + 1) * HEAD_SIZE] = rotate(
                part, turn_cos, turn_sin
            ).astype(jnp.bfloat16)


def project(order, source, slots, families, bias, cosine, sine):
    rows, half = slots[0].shape[1:]
    columns = families[0].shape[1] * (len(families) // INNER)
    in_vmem = pl.BlockSpec(memory_space=pltpu.VMEM)
    anywhere = pl.BlockSpec(memory_space=pl.ANY)
    scalars = pl.BlockSpec(memory_space=pltpu.SMEM)
    return pl.pallas_call(
        project_kernel,
        out_shape=jax.ShapeDtypeStruct((PLANES * rows, columns), jnp.bfloat16),
        in_specs=[scalars, scalars] + [anywhere] * (PLANES + len(families)) + [in_vmem] * 3,
        out_specs=in_vmem,
        scratch_shapes=[
            pltpu.VMEM((PLANES, PLANES * rows, 2 * half // PLANES), jnp.bfloat16),
            pltpu.VMEM((2 * half, columns), jnp.bfloat16),
            pltpu.VMEM((PLANES * rows, columns), jnp.float32),
            pltpu.SemaphoreType.DMA((PLANES * PLANES,)),
            pltpu.SemaphoreType.DMA((len(families) * PLANES,)),
        ],
        compiler_params=pltpu.CompilerParams(vmem_limit_bytes=VMEM_BYTES),
        cost_estimate=pl.CostEstimate(
            flops=2 * PLANES * rows * 2 * half * columns,
            transcendentals=0,
            bytes_accessed=2 * (PLANES * rows * 2 * half + 2 * half * columns),
        ),
        name="project",
    )(order, source, *slots, *families, bias, cosine, sine)


def attend_kernel(total_rows, facts, places, chunks, queries, *refs):
    pieces = refs[: 2 * INNER]
    outs = refs[2 * INNER : -3]
    key_buf, value_buf, sems = refs[-3:]
    at = pl.program_id(0)
    rows = pieces[-1].shape[0]
    heads = queries.shape[1] // HEAD_SIZE

    @pl.when(at == 0)
    def load():
        copies = []
        for p in range(INNER):
            for m in range(PLANES):
                start = pl.multiple_of(places[p * PLANES + m] * rows, rows)
                late = m == PLANES - 1
                for part, buf in ((0, key_buf), (1, value_buf)):
                    copies.append(
                        pltpu.make_async_copy(
                            pieces[p + INNER if late else p].at[
                                pl.ds(0 if late else m * rows, rows),
                                pl.ds(part * HEAD_SIZE, HEAD_SIZE),
                            ],
                            buf.at[pl.ds(start, rows), pl.ds(0, HEAD_SIZE)],
                            sems.at[(p * PLANES + m) * 2 + part],
                        )
                    )
        for copy in copies:
            copy.start()
        extra = key_buf.shape[0] - total_rows
        key_buf[total_rows:, :] = jnp.zeros((extra, HEAD_SIZE), jnp.bfloat16)
        value_buf[total_rows:, :HEAD_SIZE] = jnp.zeros((extra, HEAD_SIZE), jnp.bfloat16)
        value_buf[:, HEAD_SIZE:] = jnp.ones((key_buf.shape[0], HEAD_SIZE), jnp.bfloat16)
        for copy in copies:
            copy.wait()

    per_step = queries.shape[0] // BLK
    count = total_rows // INNER // BLK
    first_block = chunks[at] * per_step
    full_tiles = facts[count + first_block]
    exponent = HEAD_SIZE ** (-0.5) * math.log2(math.e)
    chains = [(p, j) for p in range(per_step) for j in range(heads // 2)]

    def part(p, h):
        return (slice(p * BLK, (p + 1) * BLK), slice(h * HEAD_SIZE, (h + 1) * HEAD_SIZE))

    stacked = [
        jnp.concatenate([queries[part(p, 2 * j)], queries[part(p, 2 * j + 1)]], axis=0)
        for p, j in chains
    ]
    lines = 2 * BLK

    def update(state, number, keys, values, visible):
        peak, held = state
        scores = lax.dot_general(
            stacked[number], keys, (((1,), (1,)), ((), ())), preferred_element_type=jnp.float32
        )
        if visible is not None:
            scores = jnp.where(visible, scores, NEG_FILL)
        new_peak = jnp.maximum(peak, jnp.max(scores, axis=-1, keepdims=True))
        weights = jnp.exp2((scores - new_peak) * exponent)
        factor = jnp.exp2((peak - new_peak) * exponent)
        held = held * factor + jnp.dot(
            weights.astype(jnp.bfloat16), values, preferred_element_type=jnp.float32
        )
        return new_peak, held

    def tiles(start, size, state):
        keys, values = key_buf[pl.ds(start, size), :], value_buf[pl.ds(start, size), :]
        return tuple(update(one, n, keys, values, None) for n, one in enumerate(state))

    def double_tile(t, state):
        return tiles(pl.multiple_of(t * 2 * TILE, 2 * TILE), 2 * TILE, state)

    def odd_tile(t, state):
        return tiles(pl.multiple_of((full_tiles - 1) * TILE, TILE), TILE, state)

    state = tuple(
        (
            jnp.full((lines, 1), NEG_FILL, jnp.float32),
            jnp.zeros((lines, 2 * HEAD_SIZE), jnp.float32),
        )
        for _ in chains
    )
    state = lax.fori_loop(0, full_tiles // 2, double_tile, state)
    state = lax.fori_loop(0, full_tiles % 2, odd_tile, state)
    line = lax.broadcasted_iota(jnp.int32, (lines, TILE), 0) % BLK
    column = lax.broadcasted_iota(jnp.int32, (lines, TILE), 1)
    results = []
    for number, (p, j) in enumerate(chains):
        block = facts[first_block + p]
        tail = pl.multiple_of(facts[2 * count + first_block + p] * BLK, BLK)
        keys, values = key_buf[pl.ds(tail, TILE), :], value_buf[pl.ds(tail, TILE), :]
        visible = column - line <= block * BLK - tail
        held = update(state[number], number, keys, values, visible)[1]
        done = (held[:, :HEAD_SIZE] / held[:, HEAD_SIZE:]).astype(jnp.bfloat16)
        results.append((part(p, 2 * j), done[:BLK]))
        results.append((part(p, 2 * j + 1), done[BLK:]))

    for k, out in enumerate(outs):

        @pl.when(at == k)
        def keep(out=out):
            for place, done in results:
                out[place] = done


def attend(facts, places, chunks, queries, pieces, total_rows):
    columns = queries.shape[1]
    step = queries.shape[0] // PLANES
    count = chunks.shape[0] * step

    def kernel(*refs):
        attend_kernel(total_rows, *refs)

    return pl.pallas_call(
        kernel,
        out_shape=[jax.ShapeDtypeStruct((step, columns), jnp.bfloat16)] * chunks.shape[0],
        grid_spec=pltpu.PrefetchScalarGridSpec(
            num_scalar_prefetch=3,
            grid=(chunks.shape[0],),
            in_specs=[pl.BlockSpec((step, columns), lambda i, a, b, c: (c[i], 0))]
            + [pl.BlockSpec(memory_space=pl.ANY)] * (2 * INNER),
            out_specs=[pl.BlockSpec((step, columns), lambda i, a, b, c: (0, 0))] * chunks.shape[0],
            scratch_shapes=[
                pltpu.VMEM((total_rows + TILE - BLK, HEAD_SIZE), jnp.bfloat16),
                pltpu.VMEM((total_rows + TILE - BLK, 2 * HEAD_SIZE), jnp.bfloat16),
                pltpu.SemaphoreType.DMA((INNER * PLANES * 2,)),
            ],
        ),
        compiler_params=pltpu.CompilerParams(vmem_limit_bytes=VMEM_BYTES),
        cost_estimate=pl.CostEstimate(
            flops=4 * count * columns * (total_rows // 2),
            transcendentals=count * (columns // HEAD_SIZE) * (total_rows // 2),
            bytes_accessed=4 * count * columns + 2 * total_rows * 2 * HEAD_SIZE,
        ),
        name="attend",
    )(facts, places, chunks, queries, *pieces)


def collect_kernel(places, *refs):
    pieces, out = refs[:-1], refs[-1]
    for k, piece in enumerate(pieces):
        start = pl.multiple_of(places[k], HEAD_SIZE)
        out[:, pl.ds(start, piece.shape[1])] = piece[...]


def collect(places, pieces, columns):
    in_vmem = pl.BlockSpec(memory_space=pltpu.VMEM)
    return pl.pallas_call(
        collect_kernel,
        out_shape=jax.ShapeDtypeStruct((pieces[0].shape[0], columns), jnp.bfloat16),
        in_specs=[pl.BlockSpec(memory_space=pltpu.SMEM)] + [in_vmem] * len(pieces),
        out_specs=in_vmem,
        name="collect",
    )(places, *pieces)


def by_planes(
    hidden_in,
    norm_gain,
    w_query,
    q_bias,
    w_key,
    key_bias,
    value_weight,
    value_bias,
    block_segment,
    key_blocks,
):
    devices = PLANES * INNER
    ctx_index = lax.axis_index("ctx").astype(jnp.int32)
    tp_index = lax.axis_index("tp").astype(jnp.int32)
    plane = ctx_index // INNER
    inner = ctx_index % INNER
    rows, half = hidden_in.shape
    nblocks = block_segment.shape[0]
    head_columns = w_query.shape[1] // PLANES

    def swap(array, bits):
        return lax.ppermute(array, "ctx", [(i, i ^ bits) for i in range(devices)])

    def pair_planes(array, low):
        def partner(i):
            z = i // INNER
            to = low + ((z - low) ^ 1)
            return i + (to - z) * INNER if low <= z and 0 <= to < PLANES else i

        return lax.ppermute(
            array, "ctx", [(i, partner(i)) for i in range(devices) if partner(i) != i]
        )

    def across(array):
        return lax.ppermute(array, "tp", [(0, 1), (1, 0)])

    def exchange(array):
        return lax.all_to_all(
            array,
            "ctx",
            0,
            0,
            axis_index_groups=[
                [z * INNER + r for z in range(PLANES)] for r in range(INNER)
            ],
            tiled=True,
        )

    def stacked_columns(array, stride, offset, columns):
        return [
            lax.slice_in_dim(array, z * stride + offset, z * stride + offset + columns, axis=1)
            for z in range(PLANES)
        ]

    kv_send = jnp.concatenate(
        [
            jnp.concatenate(pair, axis=1)
            for pair in zip(
                stacked_columns(w_key, HEAD_SIZE, 0, HEAD_SIZE),
                stacked_columns(value_weight, HEAD_SIZE, 0, HEAD_SIZE),
            )
        ],
        axis=0,
    )
    query_send = [
        jnp.concatenate(stacked_columns(w_query, head_columns, offset, COLUMNS), axis=0)
        for offset in range(0, head_columns, COLUMNS)
    ]
    table = jnp.asarray([[0, 1, 2, 3], [1, 0, 2, 3], [2, 3, 1, 0], [3, 2, 1, 0]], jnp.int32)
    order = lax.dynamic_index_in_dim(table, plane, 0, keepdims=False)
    bits = jnp.asarray([0, 2, 1, 3], jnp.int32)
    source = inner ^ bits

    each = jnp.arange(PLANES, dtype=jnp.int32)
    tokens = (
        (each * (INNER * rows) + inner * rows)[:, None]
        + jnp.arange(rows, dtype=jnp.int32)[None, :]
    ).reshape(-1)
    position, _ = token_facts(tokens, block_segment)
    frequencies = ROPE_THETA ** (
        -2.0 * jnp.arange(HEAD_SIZE // 2, dtype=jnp.float32) / HEAD_SIZE
    )
    angles = position.astype(jnp.float32)[:, None] * frequencies[None, :]
    cosine, sine = jnp.cos(angles), jnp.sin(angles)
    cosine = jnp.concatenate([cosine, cosine], axis=1)
    sine = jnp.concatenate([-sine, sine], axis=1)

    gain = norm_gain.reshape(2, half)
    kv_bias = jnp.concatenate(
        [
            lax.dynamic_slice_in_dim(key_bias, plane * HEAD_SIZE, HEAD_SIZE, 0),
            lax.dynamic_slice_in_dim(value_bias, plane * HEAD_SIZE, HEAD_SIZE, 0),
        ]
    ).astype(jnp.float32)[None]
    def slot(number, near, far):
        flags = jnp.stack([tp_index, order[number]])
        return do_slot(flags, source, near, far, kv_families, gain, kv_bias, cosine, sine)

    inside = (plane != 0) & (plane != PLANES - 1)
    phase = lax.optimization_barrier
    near1, swap_in = pair_planes(hidden_in, 0), pair_planes(hidden_in, 1)
    far0 = across(hidden_in)
    near1, swap_in, far0, kv_send, cosine, sine, *query_send = phase(
        (near1, swap_in, far0, kv_send, cosine, sine, *query_send)
    )

    swap_2a, swap_2b = pair_planes(swap_in, 0), pair_planes(near1, 1)
    far1 = across(near1)
    kv_a = exchange(kv_send)
    swap_in, swap_2a, swap_2b, far1, kv_a, *query_send = phase(
        (swap_in, swap_2a, swap_2b, far1, kv_a, *query_send)
    )

    swap_3 = pair_planes(swap_2b, 0)
    near2 = jnp.where(inside, swap_in, swap_2a)
    far2 = across(near2)
    kv_b, kv_c = swap(kv_a, 2), swap(kv_a, 1)
    kv_d = swap(kv_b, 1)
    q0_a = exchange(query_send[0])
    near3 = jnp.where(inside, swap_2b, swap_3)
    near3, near2, far2, kv_b, kv_c, kv_d, q0_a, *query_send = phase(
        (near3, near2, far2, kv_b, kv_c, kv_d, q0_a, *query_send)
    )

    kv_families = (kv_a, kv_b, kv_c, kv_d)
    far3 = across(near3)
    q0_b, q0_c = swap(q0_a, 2), swap(q0_a, 1)
    q1_a = exchange(query_send[1])
    early = [slot(0, hidden_in, far0), slot(1, near1, far1)]
    near2, far2, q1_a, q0_b, early = phase((near2, far2, q1_a, q0_b, early))
    q2_a = exchange(hold(query_send[2], q1_a))
    early, early_kv = zip(*early, slot(2, near2, far2))
    early_kv = [jnp.concatenate(early_kv, axis=0)]
    early_kv += [swap(early_kv[0], 2), swap(early_kv[0], 1)]
    early_kv.append(swap(early_kv[1], 1))
    q0_b, early = phase((q0_b, early))
    q0_d = swap(q0_b, 1)
    q1_b, q1_c = swap(q1_a, 2), swap(q1_a, 1)
    q1_d = swap(q1_b, 1)
    far3, near3, q0_b, q0_c, q2_a, early, *query_send = phase(
        (far3, near3, q0_b, q0_c, q2_a, early, *query_send)
    )

    last, late_kv = slot(3, near3, far3)
    slots = [*early, last]
    kv_all = [*early_kv, late_kv] + [swap(late_kv, bits) for bits in (2, 1, 3)]
    q2_b, q2_c = swap(q2_a, 2), swap(q2_a, 1)
    q3_a = exchange(query_send[3])
    places = (order[None, :] * INNER + source[:, None]).reshape(-1)

    per_rows = rows // BLK
    blocks = (
        (each * INNER + inner)[:, None] * per_rows
        + jnp.arange(per_rows, dtype=jnp.int32)[None, :]
    ).reshape(-1)
    block_ids = jnp.arange(nblocks, dtype=jnp.int32)
    same = block_segment[:, None] == block_segment[None, :]
    leading = jnp.min(jnp.where(same, block_ids[None, :], nblocks), axis=1).astype(jnp.int32)
    prompt = blocks < nblocks // 2
    per_tile = TILE // BLK
    full_tiles = jnp.where(prompt, blocks // per_tile, nblocks // 2 // per_tile)
    tail = jnp.where(prompt, blocks // per_tile * per_tile, lookup(leading, blocks))
    facts = jnp.concatenate([blocks, full_tiles, tail]).astype(jnp.int32)

    def queries_of(number, families):
        columns = w_query.shape[1] // PLANES // 2
        bias = lax.dynamic_slice_in_dim(
            q_bias, plane * head_columns + number * columns, columns, 0
        )
        return project(
            order, source, slots, families, bias.astype(jnp.float32)[None], cosine, sine
        )

    def attended_by(queries, distances):
        chunks = plane ^ jnp.asarray(distances, jnp.int32)
        return attend(facts, places, chunks, queries, kv_all, nblocks * BLK)

    queries_a = queries_of(0, (q0_a, q0_b, q0_c, q0_d, q1_a, q1_b, q1_c, q1_d))
    q2_b, q3_a, queries_a, kv_all = phase((q2_b, q3_a, queries_a, kv_all))
    q3_b, q3_c, q2_d = swap(q3_a, 2), swap(q3_a, 1), swap(q2_b, 1)
    far, near, beside, own = attended_by(queries_a, (3, 2, 1, 0))
    q3_b, far, near, beside, own = phase((q3_b, far, near, beside, own))
    q3_d = swap(q3_b, 1)
    finished = [swap(far, 3 * INNER), swap(near, 2 * INNER), swap(beside, INNER), own]
    queries_b = queries_of(1, (q2_a, q2_b, q2_c, q2_d, q3_a, q3_b, q3_c, q3_d))
    far, near = attended_by(queries_b, (3, 2))
    queries_b, far, near, finished = phase((queries_b, far, near, finished))
    finished += [swap(far, 3 * INNER), swap(near, 2 * INNER)]
    beside, own = attended_by(queries_b, (1, 0))
    beside, finished[4] = phase((beside, finished[4]))
    finished += [swap(beside, INNER), own]
    columns_at = [
        (plane ^ m) * head_columns + offset
        for offset in (0, head_columns // 2)
        for m in (3, 2, 1, 0)
    ]
    return collect(jnp.stack(columns_at), finished, w_query.shape[1])


def solution(mesh):
    placed = (
        P("ctx", "tp"),
        P(),
        P("ctx", "tp"),
        P("tp"),
        P("ctx", "tp"),
        P("tp"),
        P("ctx", "tp"),
        P("tp"),
        P(),
        P(),
    )
    planes = mesh.shape["ctx"] == PLANES * INNER and mesh.shape["tp"] == 2
    return jax.shard_map(
        by_planes if planes else local,
        mesh=mesh,
        in_specs=placed,
        out_specs=P("ctx", "tp"),
        check_vma=False,
    )
```

```python
import math

import jax
import jax.numpy as jnp
from jax import lax
from jax.experimental import pallas as pl
from jax.experimental.pallas import tpu as pltpu
from jax.sharding import PartitionSpec as P

HEAD_SIZE = 128
BLK = 128


ROPE_THETA = 1000000.0
EPSILON = 1e-06
NEG_FILL = -1e30


def rms_norm(rows, gain):
    widened = rows.astype(jnp.float32)
    mean_square = jnp.mean(widened * widened, axis=-1, keepdims=True)
    return (widened * lax.rsqrt(mean_square + EPSILON) * gain).astype(jnp.bfloat16)


def apply_rotation(vectors, token_position):
    half = vectors.shape[-1] // 2
    frequencies = ROPE_THETA ** (-2.0 * jnp.arange(half, dtype=jnp.float32) / vectors.shape[-1])
    angles = token_position.astype(jnp.float32)[:, None] * frequencies[None, :]
    cosine = jnp.cos(angles)[:, None, :]
    sine = jnp.sin(angles)[:, None, :]
    former = vectors[..., :half]
    latter = vectors[..., half:]
    return jnp.concatenate(
        [former * cosine - latter * sine, latter * cosine + former * sine], axis=-1
    )


def lookup(table, index):
    width = table.shape[0]
    hits = index[:, None] == jnp.arange(width, dtype=jnp.int32)[None, :]
    return jnp.sum(jnp.where(hits, table[None, :], 0), axis=1)


def token_facts(token_ids, block_segment):
    count = block_segment.shape[0]
    block_ids = jnp.arange(count, dtype=jnp.int32)
    same = block_segment[:, None] == block_segment[None, :]
    leading = jnp.min(jnp.where(same, block_ids[None, :], count), axis=1)
    blocks = token_ids // BLK
    segment = lookup(block_segment, blocks)
    token_position = jnp.where(
        segment == 0, token_ids, count // 2 * BLK + token_ids - lookup(leading, blocks) * BLK
    )
    return (token_position, segment)


def local(
    hidden_in,
    norm_gain,
    w_query,
    q_bias,
    w_key,
    key_bias,
    value_weight,
    value_bias,
    block_segment,
    key_blocks,
):
    rows_dev = hidden_in.shape[0]
    ctx_index = lax.axis_index("ctx")
    nblocks = block_segment.shape[0]
    heads_q = w_query.shape[1] // HEAD_SIZE
    heads_kv = w_key.shape[1] // HEAD_SIZE
    query_group = heads_q // heads_kv
    scale = HEAD_SIZE ** (-0.5)
    block_ids = jnp.arange(nblocks, dtype=jnp.int32)
    whole = lax.all_gather(hidden_in, "tp", axis=1, tiled=True)
    normed = rms_norm(whole, norm_gain)
    own_tokens = ctx_index * rows_dev + jnp.arange(rows_dev, dtype=jnp.int32)
    own_position, own_segment = token_facts(own_tokens, block_segment)
    listed = jnp.any(key_blocks[:, :, None] == block_ids[None, None, :], axis=1).astype(jnp.float32)

    def add_rows(piece):
        return jnp.dot(normed, piece, preferred_element_type=jnp.float32)

    key_total = add_rows(lax.all_gather(w_key, "ctx", axis=0, tiled=True))
    value_total = add_rows(lax.all_gather(value_weight, "ctx", axis=0, tiled=True))
    lifted = (key_total + key_bias.astype(jnp.float32)).reshape(rows_dev, heads_kv, HEAD_SIZE)
    key_matrix = (
        apply_rotation(lifted, own_position)
        .astype(jnp.bfloat16)
        .reshape(rows_dev, heads_kv * HEAD_SIZE)
    )
    value_matrix = (value_total + value_bias.astype(jnp.float32)).astype(jnp.bfloat16)
    key_matrix, value_matrix = (key_matrix, value_matrix)
    total = add_rows(lax.all_gather(w_query, "ctx", axis=0, tiled=True))
    lifted = (total + q_bias.astype(jnp.float32)).reshape(rows_dev, heads_q, HEAD_SIZE)
    queries = apply_rotation(lifted, own_position).astype(jnp.bfloat16)
    query_position, query_segment = token_facts(own_tokens, block_segment)
    query_onehot = ((own_tokens // BLK)[:, None] == block_ids[None, :]).astype(jnp.float32)
    query_listed = jnp.dot(query_onehot, listed, preferred_element_type=jnp.float32)
    arranged = (
        queries.reshape(rows_dev, heads_kv, query_group, HEAD_SIZE)
        .transpose(1, 2, 0, 3)
        .reshape(heads_kv, query_group * rows_dev, HEAD_SIZE)
    )
    initial = (
        jnp.full((heads_kv, query_group * rows_dev), NEG_FILL, jnp.float32),
        jnp.zeros((heads_kv, query_group * rows_dev), jnp.float32),
        jnp.zeros((heads_kv, query_group * rows_dev, HEAD_SIZE), jnp.float32),
    )

    def visit(state, key_tile, value_tile, tile_tokens):
        tile_blocks = tile_tokens // BLK
        tile_onehot = (tile_blocks[:, None] == block_ids[None, :]).astype(jnp.float32)
        in_list = jnp.dot(query_listed, tile_onehot.T, preferred_element_type=jnp.float32) > 0.5
        tile_segment = lookup(block_segment, tile_blocks)
        visible = in_list & (
            (query_segment[:, None] != tile_segment[None, :])
            | (tile_tokens[None, :] <= own_tokens[:, None])
        )

        def update(current):
            peak, denominator, accumulated = current
            scores = (
                jnp.einsum(
                    "gqd,kgd->gqk",
                    arranged,
                    key_tile.reshape(-1, heads_kv, HEAD_SIZE),
                    preferred_element_type=jnp.float32,
                )
                * scale
            )
            mask = jnp.tile(visible, (query_group, 1))[None]
            new_peak = jnp.maximum(peak, jnp.max(jnp.where(mask, scores, NEG_FILL), axis=-1))
            weights = jnp.where(mask, jnp.exp(scores - new_peak[..., None]), 0.0)
            factor = jnp.exp(peak - new_peak)
            denominator = denominator * factor + jnp.sum(weights, axis=-1)
            accumulated = accumulated * factor[..., None] + jnp.einsum(
                "gqk,kgd->gqd",
                weights.astype(jnp.bfloat16),
                value_tile.reshape(-1, heads_kv, HEAD_SIZE),
                preferred_element_type=jnp.float32,
            )
            return (new_peak, denominator, accumulated)

        def keep(current):
            return current

        return lax.cond(jnp.any(visible), update, keep, state)

    key_piece = lax.all_gather(key_matrix, "ctx", axis=0, tiled=True)
    value_piece = lax.all_gather(value_matrix, "ctx", axis=0, tiled=True)
    count = key_piece.shape[0]
    span = math.gcd(count, 512)
    steps = count // span

    def one_step(index, state):
        offset = index * span
        key_tile = lax.dynamic_slice_in_dim(key_piece, offset, span, 0)
        value_tile = lax.dynamic_slice_in_dim(value_piece, offset, span, 0)
        tile_tokens = 0 + offset + jnp.arange(span, dtype=jnp.int32)
        return visit(state, key_tile, value_tile, tile_tokens)

    final_state = lax.fori_loop(0, steps, one_step, initial)
    peak, denominator, accumulated = final_state
    attended = (accumulated / denominator[..., None]).reshape(
        heads_kv, query_group, rows_dev, HEAD_SIZE
    )
    attended = (
        attended.transpose(2, 0, 1, 3).reshape(rows_dev, heads_q * HEAD_SIZE).astype(jnp.bfloat16)
    )
    return attended


PLANES = 4
INNER = 4
TILE = 512
VMEM_BYTES = 60 << 20
COLUMNS = 256


def hold(value, *others):
    return lax.optimization_barrier((value,) + others)[0]


def fetch_weights(source, families, weight_buf, sems):
    depth = families[0].shape[0] // PLANES
    copies = [[] for _ in range(PLANES)]
    for f, family in enumerate(families):
        columns = family.shape[1]
        first = f // INNER * columns
        for z in range(PLANES):
            start = pl.multiple_of((z * INNER + source[f % INNER]) * depth, depth)
            copies[z].append(
                pltpu.make_async_copy(
                    family.at[pl.ds(z * depth, depth), :],
                    weight_buf.at[pl.ds(start, depth), pl.ds(first, columns)],
                    sems.at[f * PLANES + z],
                )
            )
    return copies


def rotate(part, turn_cos, turn_sin):
    return part * turn_cos + pltpu.roll(part, HEAD_SIZE // 2, 1) * turn_sin


def slot_kernel(
    flags, source, near, far, w0, w1, w2, w3, gain, bias, cosine, sine, out, kv, weight_buf, sems
):
    copies = sum(fetch_weights(source, (w0, w1, w2, w3), weight_buf, sems), [])
    for copy in copies:
        copy.start()
    rows, half = near.shape
    step = 32
    mine = flags[0]

    def chunk(i, carry):
        at = pl.multiple_of(i * step, step)
        left = near[pl.ds(at, step), :].astype(jnp.float32)
        right = far[pl.ds(at, step), :].astype(jnp.float32)
        total = jnp.sum(left * left, axis=-1, keepdims=True) + jnp.sum(
            right * right, axis=-1, keepdims=True
        )
        factor = lax.rsqrt(total * (0.5 / half) + EPSILON)
        out[mine, pl.ds(at, step), :] = (left * factor * gain[pl.ds(mine, 1), :]).astype(
            jnp.bfloat16
        )
        out[1 - mine, pl.ds(at, step), :] = (right * factor * gain[pl.ds(1 - mine, 1), :]).astype(
            jnp.bfloat16
        )
        return carry

    lax.fori_loop(0, rows // step, chunk, 0)
    for copy in copies:
        copy.wait()
    total = jnp.dot(out[0], weight_buf[:half, :], preferred_element_type=jnp.float32) + jnp.dot(
        out[1], weight_buf[half:, :], preferred_element_type=jnp.float32
    )
    total = total + bias[...]
    start = pl.multiple_of(flags[1] * rows, rows)
    key = rotate(total[:, :HEAD_SIZE], cosine[pl.ds(start, rows), :], sine[pl.ds(start, rows), :])
    kv[:, :HEAD_SIZE] = key.astype(jnp.bfloat16)
    kv[:, HEAD_SIZE:] = total[:, HEAD_SIZE:].astype(jnp.bfloat16)


def do_slot(flags, source, near, far, families, gain, bias, cosine, sine):
    rows, half = near.shape
    columns = families[0].shape[1]
    in_vmem = pl.BlockSpec(memory_space=pltpu.VMEM)
    anywhere = pl.BlockSpec(memory_space=pl.ANY)
    scalars = pl.BlockSpec(memory_space=pltpu.SMEM)
    return pl.pallas_call(
        slot_kernel,
        out_shape=(
            jax.ShapeDtypeStruct((2, rows, half), jnp.bfloat16),
            jax.ShapeDtypeStruct((rows, columns), jnp.bfloat16),
        ),
        in_specs=[scalars, scalars, in_vmem, in_vmem] + [anywhere] * INNER + [in_vmem] * 4,
        out_specs=(in_vmem, in_vmem),
        scratch_shapes=[
            pltpu.VMEM((2 * half, columns), jnp.bfloat16),
            pltpu.SemaphoreType.DMA((4 * PLANES,)),
        ],
        compiler_params=pltpu.CompilerParams(vmem_limit_bytes=VMEM_BYTES),
        cost_estimate=pl.CostEstimate(
            flops=4 * rows * half * columns,
            transcendentals=0,
            bytes_accessed=8 * rows * half + 4 * half * columns,
        ),
        name="slot",
    )(flags, source, near, far, *families, gain, bias, cosine, sine)


def project_kernel(order, source, *refs):
    slots, families = refs[:PLANES], refs[PLANES:-9]
    bias, cosine, sine, out, rows_buf, weight_buf, total, row_sems, weight_sems = refs[-9:]
    rows, half = slots[0].shape[1:]
    columns = out.shape[1]
    depth = half // PLANES
    by_plane = fetch_weights(source, families, weight_buf, weight_sems)
    near = source[0] // 2
    chunks = []
    for z in range(PLANES):
        for g in range(2):
            within = (z * 2 + (1 - near if g else near)) * depth
            chunk = [copy for f, copy in enumerate(by_plane[z]) if f % 2 == g]
            part = z * 2 * depth // half
            first = pl.multiple_of(within - part * half, depth)
            for s in range(PLANES):
                chunk.append(
                    pltpu.make_async_copy(
                        slots[s].at[part, :, pl.ds(first, depth)],
                        rows_buf.at[2 * z + g, pl.ds(s * rows, rows), :],
                        row_sems.at[(2 * z + g) * PLANES + s],
                    )
                )
            for copy in chunk:
                copy.start()
            chunks.append((chunk, pl.multiple_of(within, depth)))
    for k, (chunk, within) in enumerate(chunks):
        for copy in chunk:
            copy.wait()
        product = jnp.dot(
            rows_buf[k], weight_buf[pl.ds(within, depth), :], preferred_element_type=jnp.float32
        )
        if k == 0:
            total[...] = product
        elif k < len(chunks) - 1:
            total[...] += product
        else:
            total[...] = total[...] + product + bias[...]
    for s in range(PLANES):
        start = pl.multiple_of(order[s] * rows, rows)
        turn_cos = cosine[pl.ds(start, rows), :]
        turn_sin = sine[pl.ds(start, rows), :]
        for h in range(columns // HEAD_SIZE):
            part = total[s * rows : (s + 1) * rows, h * HEAD_SIZE : (h + 1) * HEAD_SIZE]
            out[pl.ds(start, rows), h * HEAD_SIZE : (h + 1) * HEAD_SIZE] = rotate(
                part, turn_cos, turn_sin
            ).astype(jnp.bfloat16)


def project(order, source, slots, families, bias, cosine, sine):
    rows, half = slots[0].shape[1:]
    columns = families[0].shape[1] * (len(families) // INNER)
    in_vmem = pl.BlockSpec(memory_space=pltpu.VMEM)
    anywhere = pl.BlockSpec(memory_space=pl.ANY)
    scalars = pl.BlockSpec(memory_space=pltpu.SMEM)
    return pl.pallas_call(
        project_kernel,
        out_shape=jax.ShapeDtypeStruct((PLANES * rows, columns), jnp.bfloat16),
        in_specs=[scalars, scalars] + [anywhere] * (PLANES + len(families)) + [in_vmem] * 3,
        out_specs=in_vmem,
        scratch_shapes=[
            pltpu.VMEM((2 * PLANES, PLANES * rows, half // PLANES), jnp.bfloat16),
            pltpu.VMEM((2 * half, columns), jnp.bfloat16),
            pltpu.VMEM((PLANES * rows, columns), jnp.float32),
            pltpu.SemaphoreType.DMA((2 * PLANES * PLANES,)),
            pltpu.SemaphoreType.DMA((len(families) * PLANES,)),
        ],
        compiler_params=pltpu.CompilerParams(vmem_limit_bytes=VMEM_BYTES),
        cost_estimate=pl.CostEstimate(
            flops=2 * PLANES * rows * 2 * half * columns,
            transcendentals=0,
            bytes_accessed=2 * (PLANES * rows * 2 * half + 2 * half * columns),
        ),
        name="project",
    )(order, source, *slots, *families, bias, cosine, sine)


def attend_kernel(total_rows, facts, places, chunks, queries, *refs):
    pieces = refs[: 2 * INNER]
    outs = refs[2 * INNER : -3]
    key_buf, value_buf, sems = refs[-3:]
    at = pl.program_id(0)
    rows = pieces[-1].shape[0]
    heads = queries.shape[1] // HEAD_SIZE

    @pl.when(at == 0)
    def load():
        copies = []
        for p in range(INNER):
            for m in range(PLANES):
                start = pl.multiple_of(places[p * PLANES + m] * rows, rows)
                late = m == PLANES - 1
                for part, buf in ((0, key_buf), (1, value_buf)):
                    copies.append(
                        pltpu.make_async_copy(
                            pieces[p + INNER if late else p].at[
                                pl.ds(0 if late else m * rows, rows),
                                pl.ds(part * HEAD_SIZE, HEAD_SIZE),
                            ],
                            buf.at[pl.ds(start, rows), pl.ds(0, HEAD_SIZE)],
                            sems.at[(p * PLANES + m) * 2 + part],
                        )
                    )
        for copy in copies:
            copy.start()
        extra = key_buf.shape[0] - total_rows
        key_buf[total_rows:, :] = jnp.zeros((extra, HEAD_SIZE), jnp.bfloat16)
        value_buf[total_rows:, :HEAD_SIZE] = jnp.zeros((extra, HEAD_SIZE), jnp.bfloat16)
        value_buf[:, HEAD_SIZE:] = jnp.ones((key_buf.shape[0], HEAD_SIZE), jnp.bfloat16)
        for copy in copies:
            copy.wait()

    per_step = queries.shape[0] // BLK
    count = total_rows // INNER // BLK
    first_block = chunks[at] * per_step
    full_tiles = facts[count + first_block]
    exponent = HEAD_SIZE ** (-0.5) * math.log2(math.e)
    chains = [(p, j) for p in range(per_step) for j in range(heads // 2)]

    def part(p, h):
        return (slice(p * BLK, (p + 1) * BLK), slice(h * HEAD_SIZE, (h + 1) * HEAD_SIZE))

    stacked = [
        jnp.concatenate([queries[part(p, 2 * j)], queries[part(p, 2 * j + 1)]], axis=0)
        for p, j in chains
    ]
    lines = 2 * BLK

    def update(state, number, keys, values, visible):
        peak, held = state
        scores = lax.dot_general(
            stacked[number], keys, (((1,), (1,)), ((), ())), preferred_element_type=jnp.float32
        )
        if visible is not None:
            scores = jnp.where(visible, scores, NEG_FILL)
        new_peak = jnp.maximum(peak, jnp.max(scores, axis=-1, keepdims=True))
        weights = jnp.exp2((scores - new_peak) * exponent)
        factor = jnp.exp2((peak - new_peak) * exponent)
        held = held * factor + jnp.dot(
            weights.astype(jnp.bfloat16), values, preferred_element_type=jnp.float32
        )
        return new_peak, held

    def tiles(start, size, state):
        keys, values = key_buf[pl.ds(start, size), :], value_buf[pl.ds(start, size), :]
        return tuple(update(one, n, keys, values, None) for n, one in enumerate(state))

    def double_tile(t, state):
        return tiles(pl.multiple_of(t * 2 * TILE, 2 * TILE), 2 * TILE, state)

    def odd_tile(t, state):
        return tiles(pl.multiple_of((full_tiles - 1) * TILE, TILE), TILE, state)

    state = tuple(
        (
            jnp.full((lines, 1), NEG_FILL, jnp.float32),
            jnp.zeros((lines, 2 * HEAD_SIZE), jnp.float32),
        )
        for _ in chains
    )
    state = lax.fori_loop(0, full_tiles // 2, double_tile, state)
    state = lax.fori_loop(0, full_tiles % 2, odd_tile, state)
    line = lax.broadcasted_iota(jnp.int32, (lines, TILE), 0) % BLK
    column = lax.broadcasted_iota(jnp.int32, (lines, TILE), 1)
    results = []
    for number, (p, j) in enumerate(chains):
        block = facts[first_block + p]
        tail = pl.multiple_of(facts[2 * count + first_block + p] * BLK, BLK)
        keys, values = key_buf[pl.ds(tail, TILE), :], value_buf[pl.ds(tail, TILE), :]
        visible = column - line <= block * BLK - tail
        held = update(state[number], number, keys, values, visible)[1]
        done = (held[:, :HEAD_SIZE] / held[:, HEAD_SIZE:]).astype(jnp.bfloat16)
        results.append((part(p, 2 * j), done[:BLK]))
        results.append((part(p, 2 * j + 1), done[BLK:]))

    for k, out in enumerate(outs):

        @pl.when(at == k)
        def keep(out=out):
            for place, done in results:
                out[place] = done


def attend(facts, places, chunks, queries, pieces, total_rows):
    columns = queries.shape[1]
    step = queries.shape[0] // PLANES
    count = chunks.shape[0] * step

    def kernel(*refs):
        attend_kernel(total_rows, *refs)

    return pl.pallas_call(
        kernel,
        out_shape=[jax.ShapeDtypeStruct((step, columns), jnp.bfloat16)] * chunks.shape[0],
        grid_spec=pltpu.PrefetchScalarGridSpec(
            num_scalar_prefetch=3,
            grid=(chunks.shape[0],),
            in_specs=[pl.BlockSpec((step, columns), lambda i, a, b, c: (c[i], 0))]
            + [pl.BlockSpec(memory_space=pl.ANY)] * (2 * INNER),
            out_specs=[pl.BlockSpec((step, columns), lambda i, a, b, c: (0, 0))] * chunks.shape[0],
            scratch_shapes=[
                pltpu.VMEM((total_rows + TILE - BLK, HEAD_SIZE), jnp.bfloat16),
                pltpu.VMEM((total_rows + TILE - BLK, 2 * HEAD_SIZE), jnp.bfloat16),
                pltpu.SemaphoreType.DMA((INNER * PLANES * 2,)),
            ],
        ),
        compiler_params=pltpu.CompilerParams(vmem_limit_bytes=VMEM_BYTES),
        cost_estimate=pl.CostEstimate(
            flops=4 * count * columns * (total_rows // 2),
            transcendentals=count * (columns // HEAD_SIZE) * (total_rows // 2),
            bytes_accessed=4 * count * columns + 2 * total_rows * 2 * HEAD_SIZE,
        ),
        name="attend",
    )(facts, places, chunks, queries, *pieces)


def collect_kernel(places, *refs):
    pieces, out = refs[:-1], refs[-1]
    for k, piece in enumerate(pieces):
        start = pl.multiple_of(places[k], HEAD_SIZE)
        out[:, pl.ds(start, piece.shape[1])] = piece[...]


def collect(places, pieces, columns):
    in_vmem = pl.BlockSpec(memory_space=pltpu.VMEM)
    return pl.pallas_call(
        collect_kernel,
        out_shape=jax.ShapeDtypeStruct((pieces[0].shape[0], columns), jnp.bfloat16),
        in_specs=[pl.BlockSpec(memory_space=pltpu.SMEM)] + [in_vmem] * len(pieces),
        out_specs=in_vmem,
        name="collect",
    )(places, *pieces)


def by_planes(
    hidden_in,
    norm_gain,
    w_query,
    q_bias,
    w_key,
    key_bias,
    value_weight,
    value_bias,
    block_segment,
    key_blocks,
):
    devices = PLANES * INNER
    ctx_index = lax.axis_index("ctx").astype(jnp.int32)
    tp_index = lax.axis_index("tp").astype(jnp.int32)
    plane = ctx_index // INNER
    inner = ctx_index % INNER
    rows, half = hidden_in.shape
    nblocks = block_segment.shape[0]
    head_columns = w_query.shape[1] // PLANES

    def swap(array, bits):
        return lax.ppermute(array, "ctx", [(i, i ^ bits) for i in range(devices)])

    def pair_planes(array, low):
        def partner(i):
            z = i // INNER
            to = low + ((z - low) ^ 1)
            return i + (to - z) * INNER if low <= z and 0 <= to < PLANES else i

        return lax.ppermute(
            array, "ctx", [(i, partner(i)) for i in range(devices) if partner(i) != i]
        )

    def across(array):
        return lax.ppermute(array, "tp", [(0, 1), (1, 0)])

    def exchange(array):
        return lax.all_to_all(
            array,
            "ctx",
            0,
            0,
            axis_index_groups=[
                [z * INNER + r for z in range(PLANES)] for r in range(INNER)
            ],
            tiled=True,
        )

    def stacked_columns(array, stride, offset, columns):
        return [
            lax.slice_in_dim(array, z * stride + offset, z * stride + offset + columns, axis=1)
            for z in range(PLANES)
        ]

    kv_send = jnp.concatenate(
        [
            jnp.concatenate(pair, axis=1)
            for pair in zip(
                stacked_columns(w_key, HEAD_SIZE, 0, HEAD_SIZE),
                stacked_columns(value_weight, HEAD_SIZE, 0, HEAD_SIZE),
            )
        ],
        axis=0,
    )
    query_send = [
        jnp.concatenate(stacked_columns(w_query, head_columns, offset, COLUMNS), axis=0)
        for offset in range(0, head_columns, COLUMNS)
    ]
    table = jnp.asarray([[0, 1, 2, 3], [1, 0, 2, 3], [2, 3, 1, 0], [3, 2, 1, 0]], jnp.int32)
    order = lax.dynamic_index_in_dim(table, plane, 0, keepdims=False)
    bits = jnp.asarray([0, 2, 1, 3], jnp.int32)
    source = inner ^ bits

    each = jnp.arange(PLANES, dtype=jnp.int32)
    tokens = (
        (each * (INNER * rows) + inner * rows)[:, None]
        + jnp.arange(rows, dtype=jnp.int32)[None, :]
    ).reshape(-1)
    position, _ = token_facts(tokens, block_segment)
    frequencies = ROPE_THETA ** (
        -2.0 * jnp.arange(HEAD_SIZE // 2, dtype=jnp.float32) / HEAD_SIZE
    )
    angles = position.astype(jnp.float32)[:, None] * frequencies[None, :]
    cosine, sine = jnp.cos(angles), jnp.sin(angles)
    cosine = jnp.concatenate([cosine, cosine], axis=1)
    sine = jnp.concatenate([-sine, sine], axis=1)

    gain = norm_gain.reshape(2, half)
    kv_bias = jnp.concatenate(
        [
            lax.dynamic_slice_in_dim(key_bias, plane * HEAD_SIZE, HEAD_SIZE, 0),
            lax.dynamic_slice_in_dim(value_bias, plane * HEAD_SIZE, HEAD_SIZE, 0),
        ]
    ).astype(jnp.float32)[None]
    def slot(number, near, far):
        flags = jnp.stack([tp_index, order[number]])
        return do_slot(flags, source, near, far, kv_families, gain, kv_bias, cosine, sine)

    inside = (plane != 0) & (plane != PLANES - 1)
    phase = lax.optimization_barrier
    near1, swap_in = pair_planes(hidden_in, 0), pair_planes(hidden_in, 1)
    far0 = across(hidden_in)
    near1, swap_in, far0, kv_send, cosine, sine, *query_send = phase(
        (near1, swap_in, far0, kv_send, cosine, sine, *query_send)
    )

    swap_2a, swap_2b = pair_planes(swap_in, 0), pair_planes(near1, 1)
    far1 = across(near1)
    kv_a = exchange(kv_send)
    swap_in, swap_2a, swap_2b, far1, kv_a, *query_send = phase(
        (swap_in, swap_2a, swap_2b, far1, kv_a, *query_send)
    )

    swap_3 = pair_planes(swap_2b, 0)
    near2 = jnp.where(inside, swap_in, swap_2a)
    far2 = across(near2)
    kv_b, kv_c = swap(kv_a, 2), swap(kv_a, 1)
    kv_d = swap(kv_b, 1)
    q0_a = exchange(query_send[0])
    near3 = jnp.where(inside, swap_2b, swap_3)
    near3, near2, far2, kv_b, kv_c, kv_d, q0_a, *query_send = phase(
        (near3, near2, far2, kv_b, kv_c, kv_d, q0_a, *query_send)
    )

    kv_families = (kv_a, kv_b, kv_c, kv_d)
    far3 = across(near3)
    q0_b, q0_c = swap(q0_a, 2), swap(q0_a, 1)
    q1_a = exchange(query_send[1])
    early = [slot(0, hidden_in, far0), slot(1, near1, far1)]
    near2, far2, q1_a, q0_b, early = phase((near2, far2, q1_a, q0_b, early))
    q2_a = exchange(hold(query_send[2], q1_a))
    early, early_kv = zip(*early, slot(2, near2, far2))
    early_kv = [jnp.concatenate(early_kv, axis=0)]
    early_kv += [swap(early_kv[0], 2), swap(early_kv[0], 1)]
    early_kv.append(swap(early_kv[1], 1))
    q0_b, early = phase((q0_b, early))
    q0_d = swap(q0_b, 1)
    q1_b, q1_c = swap(q1_a, 2), swap(q1_a, 1)
    q1_d = swap(q1_b, 1)
    far3, near3, q0_b, q0_c, q2_a, early, *query_send = phase(
        (far3, near3, q0_b, q0_c, q2_a, early, *query_send)
    )

    last, late_kv = slot(3, near3, far3)
    slots = [*early, last]
    kv_all = [*early_kv, late_kv] + [swap(late_kv, bits) for bits in (2, 1, 3)]
    q2_b, q2_c = swap(q2_a, 2), swap(q2_a, 1)
    q3_a = exchange(query_send[3])
    places = (order[None, :] * INNER + source[:, None]).reshape(-1)

    per_rows = rows // BLK
    blocks = (
        (each * INNER + inner)[:, None] * per_rows
        + jnp.arange(per_rows, dtype=jnp.int32)[None, :]
    ).reshape(-1)
    block_ids = jnp.arange(nblocks, dtype=jnp.int32)
    same = block_segment[:, None] == block_segment[None, :]
    leading = jnp.min(jnp.where(same, block_ids[None, :], nblocks), axis=1).astype(jnp.int32)
    prompt = blocks < nblocks // 2
    per_tile = TILE // BLK
    full_tiles = jnp.where(prompt, blocks // per_tile, nblocks // 2 // per_tile)
    tail = jnp.where(prompt, blocks // per_tile * per_tile, lookup(leading, blocks))
    facts = jnp.concatenate([blocks, full_tiles, tail]).astype(jnp.int32)

    def queries_of(number, families):
        columns = w_query.shape[1] // PLANES // 2
        bias = lax.dynamic_slice_in_dim(
            q_bias, plane * head_columns + number * columns, columns, 0
        )
        return project(
            order, source, slots, families, bias.astype(jnp.float32)[None], cosine, sine
        )

    def attended_by(queries, distances):
        chunks = plane ^ jnp.asarray(distances, jnp.int32)
        return attend(facts, places, chunks, queries, kv_all, nblocks * BLK)

    queries_a = queries_of(0, (q0_a, q0_b, q0_c, q0_d, q1_a, q1_b, q1_c, q1_d))
    q2_b, q3_a, queries_a, kv_all = phase((q2_b, q3_a, queries_a, kv_all))
    q3_b, q3_c, q2_d = swap(q3_a, 2), swap(q3_a, 1), swap(q2_b, 1)
    far, near, beside, own = attended_by(queries_a, (3, 2, 1, 0))
    q3_b, far, near, beside, own = phase((q3_b, far, near, beside, own))
    q3_d = swap(q3_b, 1)
    finished = [swap(far, 3 * INNER), swap(near, 2 * INNER), swap(beside, INNER), own]
    queries_b = queries_of(1, (q2_a, q2_b, q2_c, q2_d, q3_a, q3_b, q3_c, q3_d))
    far, near = attended_by(queries_b, (3, 2))
    queries_b, far, near, finished = phase((queries_b, far, near, finished))
    finished += [swap(far, 3 * INNER), swap(near, 2 * INNER)]
    beside, own = attended_by(queries_b, (1, 0))
    finished += [swap(beside, INNER), own]
    columns_at = [
        (plane ^ m) * head_columns + offset
        for offset in (0, head_columns // 2)
        for m in (3, 2, 1, 0)
    ]
    return collect(jnp.stack(columns_at), finished, w_query.shape[1])


def solution(mesh):
    placed = (
        P("ctx", "tp"),
        P(),
        P("ctx", "tp"),
        P("tp"),
        P("ctx", "tp"),
        P("tp"),
        P("ctx", "tp"),
        P("tp"),
        P(),
        P(),
    )
    planes = mesh.shape["ctx"] == PLANES * INNER and mesh.shape["tp"] == 2
    return jax.shard_map(
        by_planes if planes else local,
        mesh=mesh,
        in_specs=placed,
        out_specs=P("ctx", "tp"),
        check_vma=False,
    )
```
